32 devices in a mesh: dp: 8 (over z, y), own: 4 (over x, core).
Axes of the slice: x: 2, y: 2, z: 4, core: 2. Of those that a mesh axis runs over, the one named last changes fastest.
Arguments:
- acts_kv: bfloat16 [1024, 2560], P('dp', 'own'), may hold values from -6 to 6
- grads_kv: bfloat16 [1024, 1024], P('dp', 'own'), may hold values from -6 to 6
- acts_up: bfloat16 [1024, 2560], P('dp', 'own'), may hold values from -6 to 6
- grads_up: bfloat16 [1024, 3072], P('dp', 'own'), may hold values from -6 to 6
- prev_a_kv: float32 [4, 640, 640], P('own'), as said below
- prev_g_kv: float32 [4, 256, 256], P('own'), as said below
- prev_a_up: float32 [4, 640, 640], P('own'), as said below
- prev_g_up: float32 [4, 768, 768], P('own'), as said below
- owners: int32 [2, 4], replicated, may hold values from 0 to 7, as said below
- damping: float32 [4], replicated, may hold values from 0.05 to 0.5
- init_scale: float32 [4, 4], replicated, may hold values from 0.4 to 0.8
- weights_kv: float32 [2560, 1024], P('own', 'dp'), may hold values from -0.75 to 0.75
- weights_up: float32 [2560, 3072], P('own', 'dp'), may hold values from -0.75 to 0.75
- step_size: float32 [], replicated, may hold values from 0.2 to 0.5
Outputs:
- new_kv: float32 [2560, 1024], P('own', 'dp')
- new_up: float32 [2560, 3072], P('own', 'dp')
The draws below stay inside these ranges and needn't reach their ends.
Inputs may be any that keep to these rules, and one draw needn't show every extreme that they name: `owners`: row 0 names for each factor the dp index that inverts it: one index is named by two factors, the others by one, and 0 and 7 are always named. Row 1 refreshes both factors of one of the two linears and leaves at least one factor of the other unrefreshed. `prev_a_kv`: every block is symmetric and positive definite. `prev_g_kv`: every block is symmetric and positive definite. `prev_a_up`: every block is symmetric and positive definite. `prev_g_up`: every block is symmetric and positive definite.
All inputs are finite; a program needn't handle non-finite values.
Results may differ from the reference program's by a relative error of at most 0.0021.
Values may be sent and summed in bfloat16 or wider, within the bound.
No kernel may reach another device: no remote copies, remote signals or barrier semaphores. Data moves between devices by JAX's collectives and lax.ppermute only.
A program may use at most 128 MiB of HBM per device.

```python
import math
import jax
import jax.numpy as jnp
from jax import lax

D = 2560
OUT_KV = 1024
OUT_UP = 3072
BLOCKS = 4
NF = 4
NS_STEPS = 2
TOKENS = 1024
N_DP = 8


def spd_blocks(key, count, block_width):
    noise_key, diag_key = jax.random.split(key)
    noise = jax.random.normal(noise_key, (count, block_width, block_width), jnp.float32)
    symmetric = (noise + jnp.swapaxes(noise, 1, 2)) * (0.5 / math.sqrt(2.0 * block_width))
    diagonal = jnp.exp(jax.random.uniform(diag_key, (count, block_width, 1), jnp.float32, math.log(1.5), math.log(3.0)))
    identity = jnp.eye(block_width, dtype=jnp.float32)
    return symmetric * (1.0 - identity) + diagonal * identity


def draw_prev_a_kv(key, part):
    return spd_blocks(jax.random.fold_in(key, 11), BLOCKS, D // BLOCKS)


def draw_prev_g_kv(key, part):
    return spd_blocks(jax.random.fold_in(key, 12), BLOCKS, OUT_KV // BLOCKS)


def draw_prev_a_up(key, part):
    return spd_blocks(jax.random.fold_in(key, 13), BLOCKS, D // BLOCKS)


def draw_prev_g_up(key, part):
    return spd_blocks(jax.random.fold_in(key, 14), BLOCKS, OUT_UP // BLOCKS)


def draw_owners(key, part):
    keys = jax.random.split(jax.random.fold_in(key, 21), 5)
    shared = jax.random.randint(keys[0], (), 1, N_DP - 1)
    listed = jnp.stack([jnp.zeros((), jnp.int32), jnp.full((), N_DP - 1, jnp.int32), shared, shared])
    order = jax.random.permutation(keys[1], NF)
    owner_row = listed[order]
    fresh_linear = jax.random.randint(keys[2], (), 0, 2)
    other_factor = 2 * (1 - fresh_linear) + jax.random.randint(keys[3], (), 0, 2)
    other_flag = jax.random.randint(keys[4], (), 0, 2)
    factor_ids = jnp.arange(NF, dtype=jnp.int32)
    flags = (factor_ids // 2 == fresh_linear).astype(jnp.int32)
    flags = jnp.where(factor_ids == other_factor, other_flag, flags)
    return jnp.stack([owner_row.astype(jnp.int32), flags.astype(jnp.int32)]).astype(jnp.int32)


def steps_of(rng, extent, pieces, smallest, largest):
    loudness = 1.0
    for dim, blocks in pieces:
        steps = jax.random.uniform(jax.random.fold_in(jax.random.fold_in(rng, 6), dim), (blocks,), jnp.float32, smallest / len(pieces), largest / len(pieces))
        loudness = loudness * jnp.repeat(jnp.exp(steps), extent[dim] // blocks).reshape((-1,) + (1,) * (len(extent) - 1 - dim))
    return loudness


def scatter_about(own_key, extent, deviation, limit, cuts=(), kind=jnp.bfloat16):
    values = jax.random.normal(own_key, extent, jnp.float32) * deviation
    if len(cuts) > 0:
        values = steps_of(own_key, extent, cuts, -0.22, 0.18) * values
    return jnp.clip(values, min=-limit, max=limit).astype(kind)


def setup_inputs(seed: int = 0) -> dict:
    key_of = jax.random.split(jax.random.key(seed), 15)
    return {
        "acts_kv": scatter_about(key_of[0], (TOKENS, D), 1.0, 6.0, ((0, 8), (1, 4))),
        "grads_kv": scatter_about(key_of[1], (TOKENS, OUT_KV), 1.0, 6.0, ((0, 8), (1, 4))),
        "acts_up": scatter_about(key_of[2], (TOKENS, D), 1.0, 6.0, ((0, 8), (1, 4))),
        "grads_up": scatter_about(key_of[3], (TOKENS, OUT_UP), 1.0, 6.0, ((0, 8), (1, 4))),
        "prev_a_kv": draw_prev_a_kv(jax.random.fold_in(key_of[14], 71), 0),
        "prev_g_kv": draw_prev_g_kv(jax.random.fold_in(key_of[14], 71), 0),
        "prev_a_up": draw_prev_a_up(jax.random.fold_in(key_of[14], 71), 0),
        "prev_g_up": draw_prev_g_up(jax.random.fold_in(key_of[14], 71), 0),
        "owners": draw_owners(jax.random.fold_in(key_of[14], 71), 0),
        "damping": jnp.clip(jnp.exp(jax.random.uniform(key_of[9], (NF,), jnp.float32, math.log(0.05), math.log(0.5))), 0.05, 0.5),
        "init_scale": jnp.clip(jax.random.uniform(key_of[10], (NF, BLOCKS), jnp.float32, 0.4, 0.8), 0.4, 0.8),
        "weights_kv": scatter_about(key_of[11], (D, OUT_KV), 0.05, 0.75, ((0, 4), (1, 8)), jnp.float32),
        "weights_up": scatter_about(key_of[12], (D, OUT_UP), 0.05, 0.75, ((0, 4), (1, 8)), jnp.float32),
        "step_size": jnp.clip(jax.random.uniform(key_of[13], (), jnp.float32, 0.2, 0.5), 0.2, 0.5),
    }


def matrix_product(left_side, right_side):
    return jnp.dot(left_side, right_side, preferred_element_type=jnp.float32, precision=lax.Precision.HIGHEST)

def spd_inverse(previous, summed, fresh, damping_value, scale_value):
    block_width = previous.shape[0]
    identity = jnp.eye(block_width, dtype=jnp.float32)
    damped = jnp.where(fresh == 1, 0.5 * previous + 0.5 * summed, previous) + damping_value * identity
    frobenius = jnp.sqrt(jnp.sum(damped * damped))
    iterate = scale_value / frobenius * identity
    for repeat in range(NS_STEPS):
        iterate = 2.0 * iterate - matrix_product(matrix_product(damped, iterate), iterate)
    return iterate.astype(jnp.bfloat16)

def factor_inverses(values, previous, fresh, damping_value, scales):
    block_width = previous.shape[1]
    token_total = values.shape[0]
    outputs = []
    for block_index in range(BLOCKS):
        column_block = values[:, block_index * block_width:(block_index + 1) * block_width]
        summed = jnp.dot(column_block.T, column_block, preferred_element_type=jnp.float32) / token_total
        outputs.append(spd_inverse(previous[block_index], summed, fresh, damping_value, scales[block_index]))
    return outputs

def block_diagonal(blocks):
    block_width = blocks[0].shape[0]
    full_width = block_width * len(blocks)
    matrix = jnp.zeros((full_width, full_width), blocks[0].dtype)
    for block_index in range(len(blocks)):
        offset = block_index * block_width
        matrix = matrix.at[offset:offset + block_width, offset:offset + block_width].set(blocks[block_index])
    return matrix

def layer_update(activations, out_grads, left_blocks, right_blocks, weights, step_size, entries):
    gradient = jnp.dot(activations.T, out_grads, preferred_element_type=jnp.float32) / activations.shape[0]
    grad_low = gradient.astype(jnp.bfloat16)
    right_part = jnp.dot(grad_low, block_diagonal(right_blocks), preferred_element_type=jnp.float32).astype(jnp.bfloat16)
    precond = jnp.dot(block_diagonal(left_blocks), right_part, preferred_element_type=jnp.float32)
    quadratic = jnp.sum(precond * grad_low.astype(jnp.float32))
    return weights - step_size * jnp.sqrt(entries / quadratic) * precond

def reference(acts_kv, grads_kv, acts_up, grads_up, prev_a_kv, prev_g_kv, prev_a_up, prev_g_up, owners, damping, init_scale, weights_kv, weights_up, step_size):
    inv_a_kv = factor_inverses(acts_kv, prev_a_kv, owners[1, 0], damping[0], init_scale[0])
    inv_g_kv = factor_inverses(grads_kv, prev_g_kv, owners[1, 1], damping[1], init_scale[1])
    inv_a_up = factor_inverses(acts_up, prev_a_up, owners[1, 2], damping[2], init_scale[2])
    inv_g_up = factor_inverses(grads_up, prev_g_up, owners[1, 3], damping[3], init_scale[3])
    new_kv = layer_update(acts_kv, grads_kv, inv_a_kv, inv_g_kv, weights_kv, step_size, D * OUT_KV)
    new_up = layer_update(acts_up, grads_up, inv_a_up, inv_g_up, weights_up, step_size, D * OUT_UP)
    return (new_kv, new_up)
```

```python
import jax
import jax.numpy as jnp
from jax import lax
from jax.sharding import PartitionSpec as P

BF = jnp.bfloat16
F32 = jnp.float32


def mm(a, b, dims=((1,), (0,))):
    return lax.dot_general(a, b, (dims, ((), ())), preferred_element_type=F32)


def damp(previous, stat, fresh, lam):
    n = previous.shape[0]
    eye = (lax.broadcasted_iota(jnp.int32, (n, n), 0) == lax.broadcasted_iota(jnp.int32, (n, n), 1))
    mixed = jnp.where(fresh == 1, 0.5 * previous + 0.5 * stat, previous)
    return mixed + jnp.where(eye, lam, 0.0)


def normalised(damped, scale):
    coef = scale / jnp.sqrt(jnp.sum(damped * damped))
    return coef, coef * damped


def inverse_columns(damped, scale, start, width):
    n = damped.shape[0]
    coef, y_full = normalised(damped, scale)
    y_low = y_full.astype(BF)
    y_cols = lax.dynamic_slice_in_dim(y_full, start, width, 1)
    square = mm(y_low, y_cols.astype(BF))
    cubic = mm(y_low, (4.0 * y_cols - square).astype(BF))
    rows = lax.broadcasted_iota(jnp.int32, (n, width), 0)
    cols = lax.broadcasted_iota(jnp.int32, (n, width), 1) + start
    out = coef * (jnp.where(rows == cols, 4.0, 0.0) - 6.0 * y_cols + cubic)
    return out.astype(BF)


def apply_inverse(damped, scale, right):
    coef, y_full = normalised(damped, scale)
    y_low = y_full.astype(BF)
    wide = right.astype(F32)
    inner = 4.0 * wide - mm(y_low, right)
    inner = 6.0 * wide - mm(y_low, inner.astype(BF))
    return coef * (4.0 * wide - mm(y_low, inner.astype(BF)))


def gather_fast(acts, grads, prev_low):
    dp, own = lax.axis_index("dp"), lax.axis_index("own")
    z, x = dp // 2, own // 2
    rows = acts.shape[0]
    half = rows // 2
    z_swap = lambda k: [(d, d ^ (2 * k)) for d in range(8)]
    y_swap = [(d, d ^ 1) for d in range(8)]
    x_swap = [(o, o ^ 2) for o in range(4)]
    both = ("dp", "own")
    at = lambda d, o: d * 4 + o

    keep = lax.dynamic_slice_in_dim(grads, half * x, half, 0)
    give = lax.dynamic_slice_in_dim(grads, half * (1 - x), half, 0)
    take = lax.ppermute(give, "own", x_swap)
    mine = jnp.concatenate(
        [lax.dynamic_slice_in_dim(acts, half * x, half, 0), lax.dynamic_slice_in_dim(acts, half * (1 - x), half, 0)], 0
    )
    a = [mine] + [lax.ppermute(mine, "dp", z_swap(k)) for k in (1, 2, 3)]
    pieces = []
    for k in range(4):
        target = jnp.bitwise_xor(z, k)
        piece = jnp.where(target // 2 == x, keep, take)
        if k:
            pairs = [
                (at(d, o), at(d ^ (2 * k), o))
                for d in range(8)
                for o in range(4)
                if (o & 1) == (((d // 2) ^ k) & 1)
            ]
            piece = lax.ppermute(piece, both, pairs)
        pieces.append(piece)
    sender = [(d, o) for d in range(8) for o in range(4) if (o & 1) == ((d // 2) & 1)]
    near = jnp.concatenate(pieces, 0)
    far = lax.ppermute(near, both, [(at(d, o), at(d ^ 1, o)) for d, o in sender])
    row = jnp.concatenate([near, far], 0)
    across = lax.ppermute(row, both, [(at(d, o), at(d, o ^ 2)) for d, o in sender])
    block = jnp.concatenate([row, across], 0)
    copy = lax.ppermute(block, both, [(at(d, o), at(d, o ^ 1)) for d, o in sender])
    is_sender = (own & 1) == (z & 1)
    block = jnp.where(is_sender, block, copy)
    a = a + [lax.ppermute(v, "dp", y_swap) for v in a]
    acts_all = jnp.concatenate([v[:half] for v in a] + [v[half:] for v in a], 0)

    prevs = []
    for p in prev_low:
        q = lax.ppermute(p, both, [(at(d, d // 2), at(d, (d // 2) ^ 2)) for d in range(8)])
        p = jnp.where(own == z, p, q)
        q = lax.ppermute(
            p, both, [(at(d, o), at(d, o ^ 1)) for d in range(8) for o in range(4) if (o & 1) == ((d // 2) & 1)]
        )
        prevs.append(jnp.where(is_sender, p, q))
    return acts_all, block, prevs


def gather_any(acts, grads, prev_low, block_index, dp_count, own_count):
    rows, cols = grads.shape
    acts_all = lax.all_gather(acts, "dp", axis=0, tiled=True)
    split = lax.all_to_all(grads.reshape(own_count, rows // own_count, cols), "own", 0, 0, tiled=True)
    wanted = jnp.repeat(split, dp_count // own_count, axis=0)
    pieces = lax.all_to_all(wanted, "dp", 0, 0, tiled=True)
    block = lax.all_gather(pieces, "own", axis=1, tiled=True).reshape(rows * dp_count, cols)
    prevs = [
        lax.dynamic_index_in_dim(lax.all_gather(p[None], "own", axis=0, tiled=True), block_index, 0, keepdims=False)
        for p in prev_low
    ]
    return acts_all, block, prevs


def shards(acts_kv, grads_kv, acts_up, grads_up, prev_a_kv, prev_g_kv, prev_a_up, prev_g_up, owners, damping,
           init_scale, weights_kv, weights_up, step_size):
    dp_count, own_count = lax.axis_size("dp"), lax.axis_size("own")
    dp, own = lax.axis_index("dp"), lax.axis_index("own")
    block_index = dp * own_count // dp_count
    total = acts_kv.shape[0] * dp_count
    in_width = acts_kv.shape[1]
    kv_width, up_width = grads_kv.shape[1], grads_up.shape[1]
    kv_cols, up_cols = weights_kv.shape[1], weights_up.shape[1]
    slot = dp % (dp_count // own_count)

    acts = jnp.concatenate([acts_kv, acts_up], 1)
    grads = jnp.concatenate([grads_kv, grads_up], 1)
    prev_low = [prev_g_kv[0].astype(BF), prev_g_up[0].astype(BF)]
    if (dp_count, own_count) == (8, 4):
        acts_all, block, prevs = gather_fast(acts, grads, prev_low)
    else:
        acts_all, block, prevs = gather_any(acts, grads, prev_low, block_index, dp_count, own_count)

    tokens = ((0,), (0,))
    outs, terms = [], []
    for linear, (a_prev, cols, start, width) in enumerate(
        ((prev_a_kv, kv_cols, 0, kv_width), (prev_a_up, up_cols, kv_width, up_width))
    ):
        fa, fg = 2 * linear, 2 * linear + 1
        a_l = acts_all[:, linear * in_width:(linear + 1) * in_width]
        g_l = block[:, start:start + width]
        g_damped = damp(prevs[linear].astype(F32), mm(g_l, g_l, tokens) / total, owners[1, fg], damping[fg])
        g_inv = inverse_columns(g_damped, init_scale[fg, block_index], slot * cols, cols)
        low = (mm(a_l, g_l, tokens) / total).astype(BF)
        right = mm(low, g_inv).astype(BF)
        a_damped = damp(a_prev[0], mm(a_l, a_l, tokens) / total, owners[1, fa], damping[fa])
        precond = apply_inverse(a_damped, init_scale[fa, own], right)
        term = jnp.sum(precond * lax.dynamic_slice_in_dim(low, slot * cols, cols, 1).astype(F32))
        outs.append(precond)
        terms.append(term)
    lane = lax.broadcasted_iota(jnp.int32, (dp_count * own_count, 128), 1)
    packed = jnp.where(lane == 0, terms[0], jnp.where(lane == 1, terms[1], 0.0))
    totals = jnp.sum(lax.all_to_all(packed, ("dp", "own"), 0, 0, tiled=True), axis=0)
    new = []
    for linear, w in enumerate((weights_kv, weights_up)):
        entries = w.shape[0] * w.shape[1] * dp_count * own_count
        new.append(w - step_size * jnp.sqrt(entries / totals[linear]) * outs[linear])
    return tuple(new)


def solution(mesh):
    tok, fac, rep = P("dp", "own"), P("own", None, None), P()
    return jax.shard_map(
        shards,
        mesh=mesh,
        in_specs=(tok, tok, tok, tok, fac, fac, fac, fac, rep, rep, rep, P("own", "dp"), P("own", "dp"), rep),
        out_specs=(P("own", "dp"), P("own", "dp")),
        check_vma=False,
    )
```

```python
import functools

import jax
import jax.numpy as jnp
from jax import lax
from jax.experimental import pallas as pl
from jax.experimental.pallas import tpu as pltpu
from jax.sharding import PartitionSpec as P

BF = jnp.bfloat16
F32 = jnp.float32


def contract(a, b, ad, bd):
    return lax.dot_general(a, b, (((ad,), (bd,)), ((), ())), preferred_element_type=F32)


def tiles(n, step=256):
    return [(s, min(step, n - s)) for s in range(0, n, step)]


def damped_into(m_ref, product, prev_ref, keep, mix, lam):
    n = m_ref.shape[0]
    total = jnp.zeros((1, 1), F32)
    for s, w in tiles(n):
        m = keep * prev_ref[:, s:s + w].astype(F32) + mix * product(s, w)
        rows = lax.broadcasted_iota(jnp.int32, (n, w), 0)
        cols = lax.broadcasted_iota(jnp.int32, (n, w), 1) + s
        m = jnp.where(rows == cols, m + lam, m)
        m_ref[:, s:s + w] = m
        total = total + jnp.sum(m * m, keepdims=True)
    return total


def scaled_into(y_ref, m_ref, coef):
    for s, w in tiles(m_ref.shape[0]):
        y_ref[:, s:s + w] = (coef * m_ref[:, s:s + w]).astype(BF)


def tile_kernel(count, quarters, in_width, widths, sc, where_ref, *refs):
    parts, blocks = refs[:count], refs[count:count + quarters]
    pa_kv, pa_up, pg_kv, pg_up, o_kv, o_up, t_ref = refs[count + quarters:count + quarters + 7]
    at, g, m_a, y_a, low, rt = refs[count + quarters + 7:count + quarters + 13]
    factor_refs = refs[count + quarters + 13:]
    dp, slot = where_ref[0], where_ref[1]
    chunk = parts[0].shape[1]
    piece = chunk // quarters
    for m in range(count):
        at[:, chunk * m:chunk * (m + 1)] = parts[m][...]
        source = pl.multiple_of(jnp.bitwise_xor(dp, m) * piece, piece)
        for q in range(quarters):
            g[chunk * m + piece * q:chunk * m + piece * (q + 1), :] = blocks[q][pl.ds(source, piece), :]
    begin = 0
    for linear, (pa, pg, out) in enumerate(((pa_kv, pg_kv, o_kv), (pa_up, pg_up, o_up))):
        width, cols = widths[linear], out.shape[1]
        m_g, y_g, i_g = factor_refs[3 * linear:3 * linear + 3]
        fa, fg = 2 * linear, 2 * linear + 1
        part = lambda s, w, begin=begin: g[:, begin + s:begin + s + w]
        squares = damped_into(
            m_g, lambda s, w: contract(part(0, width), part(s, w), 0, 0), pg, sc[0, fg], sc[1, fg], sc[2, fg]
        )
        coef = sc[3, fg] * lax.rsqrt(squares)
        scaled_into(y_g, m_g, coef)
        first = pl.multiple_of(slot * cols, 128)
        for s, w in tiles(cols):
            yc = coef * m_g[:, pl.ds(pl.multiple_of(first + s, 128), w)]
            square = contract(y_g[...], yc.astype(BF), 1, 0)
            cubic = contract(y_g[...], (4.0 * yc - square).astype(BF), 1, 0)
            rows = lax.broadcasted_iota(jnp.int32, (width, w), 0)
            lanes = lax.broadcasted_iota(jnp.int32, (width, w), 1) + (first + s)
            i_g[:, s:s + w] = (coef * (jnp.where(rows == lanes, 4.0, 0.0) - 6.0 * yc + cubic)).astype(BF)
        al = at.at[in_width * linear:in_width * (linear + 1), :]
        for s, w in tiles(width):
            low[:, s:s + w] = (contract(al[...], part(s, w), 1, 0) * sc[4, 0]).astype(BF)
        for s, w in tiles(cols):
            rt[:, s:s + w] = contract(low[:, :width], i_g[:, s:s + w], 1, 0).astype(BF)
        squares = damped_into(
            m_a, lambda s, w: contract(al[...], al[s:s + w, :], 1, 1), pa, sc[0, fa], sc[1, fa], sc[2, fa]
        )
        coef = sc[3, fa] * lax.rsqrt(squares)
        scaled_into(y_a, m_a, coef)
        total = jnp.zeros((1, 1), F32)
        for s, w in tiles(cols):
            right = rt[:, s:s + w]
            wide = right.astype(F32)
            inner = 4.0 * wide - contract(y_a[...], right, 1, 0)
            inner = 6.0 * wide - contract(y_a[...], inner.astype(BF), 1, 0)
            pre = coef * (4.0 * wide - contract(y_a[...], inner.astype(BF), 1, 0))
            out[:, s:s + w] = pre
            own_low = low[:, pl.ds(pl.multiple_of(first + s, 128), w)].astype(F32)
            total = total + jnp.sum(pre * own_low, keepdims=True)
        t_ref[linear:linear + 1, :] = jnp.broadcast_to(total, (1, 128))
        begin += width


def tile(sc, where, parts, blocks, pa_kv, pa_up, pg_kv, pg_up, cols):
    count, quarters = len(parts), len(blocks)
    in_width, widths = pa_kv.shape[0], (pg_kv.shape[0], pg_up.shape[0])
    tokens = parts[0].shape[1] * count
    vmem, smem = pl.BlockSpec(memory_space=pltpu.VMEM), pl.BlockSpec(memory_space=pltpu.SMEM)
    factors = []
    for w, c in zip(widths, cols):
        factors += [pltpu.VMEM((w, w), F32), pltpu.VMEM((w, w), BF), pltpu.VMEM((w, c), BF)]
    return pl.pallas_call(
        functools.partial(tile_kernel, count, quarters, in_width, widths),
        out_shape=(
            jax.ShapeDtypeStruct((in_width, cols[0]), F32),
            jax.ShapeDtypeStruct((in_width, cols[1]), F32),
            jax.ShapeDtypeStruct((2, 128), F32),
        ),
        in_specs=[smem, smem] + [vmem] * (count + quarters + 4),
        out_specs=(vmem, vmem, vmem),
        scratch_shapes=[
            pltpu.VMEM((2 * in_width, tokens), BF),
            pltpu.VMEM((tokens, sum(widths)), BF),
            pltpu.VMEM((in_width, in_width), F32),
            pltpu.VMEM((in_width, in_width), BF),
            pltpu.VMEM((in_width, max(widths)), BF),
            pltpu.VMEM((in_width, max(cols)), BF),
        ]
        + factors,
        compiler_params=pltpu.CompilerParams(vmem_limit_bytes=44 * 2**20),
        name="tile",
    )(sc, where, *parts, *blocks, pa_kv, pa_up, pg_kv, pg_up)


def update_kernel(entries, step_ref, sums_ref, p_kv, p_up, w_kv, w_up, n_kv, n_up):
    totals = jnp.sum(sums_ref[...], axis=0, keepdims=True)
    for linear, (p, w, n) in enumerate(((p_kv, w_kv, n_kv), (p_up, w_up, n_up))):
        total = totals[:, 128 * linear:128 * (linear + 1)]
        factor = step_ref[0] * jnp.sqrt(entries[linear] / total)
        for s, width in tiles(p.shape[1], 128):
            n[:, s:s + width] = w[:, s:s + width] - factor[:, :width] * p[:, s:s + width]


def update(entries, step_size, sums, p_kv, p_up, w_kv, w_up):
    vmem, smem = pl.BlockSpec(memory_space=pltpu.VMEM), pl.BlockSpec(memory_space=pltpu.SMEM)
    return pl.pallas_call(
        functools.partial(update_kernel, entries),
        out_shape=(jax.ShapeDtypeStruct(w_kv.shape, F32), jax.ShapeDtypeStruct(w_up.shape, F32)),
        in_specs=[smem] + [vmem] * 5,
        out_specs=(vmem, vmem),
        name="update",
    )(step_size.reshape(1), sums, p_kv, p_up, w_kv, w_up)


def mm(a, b, dims=((1,), (0,))):
    return lax.dot_general(a, b, (dims, ((), ())), preferred_element_type=F32)


def damp(previous, stat, fresh, lam):
    n = previous.shape[0]
    eye = lax.broadcasted_iota(jnp.int32, (n, n), 0) == lax.broadcasted_iota(jnp.int32, (n, n), 1)
    mixed = jnp.where(fresh == 1, 0.5 * previous + 0.5 * stat, previous)
    return mixed + jnp.where(eye, lam, 0.0)


def normalised(damped, scale):
    coef = scale / jnp.sqrt(jnp.sum(damped * damped))
    return coef, coef * damped


def inverse_columns(damped, scale, start, width):
    n = damped.shape[0]
    coef, y_full = normalised(damped, scale)
    y_low = y_full.astype(BF)
    y_cols = lax.dynamic_slice_in_dim(y_full, start, width, 1)
    square = mm(y_low, y_cols.astype(BF))
    cubic = mm(y_low, (4.0 * y_cols - square).astype(BF))
    rows = lax.broadcasted_iota(jnp.int32, (n, width), 0)
    cols = lax.broadcasted_iota(jnp.int32, (n, width), 1) + start
    out = coef * (jnp.where(rows == cols, 4.0, 0.0) - 6.0 * y_cols + cubic)
    return out.astype(BF)


def apply_inverse(damped, scale, right):
    coef, y_full = normalised(damped, scale)
    y_low = y_full.astype(BF)
    wide = right.astype(F32)
    inner = 4.0 * wide - mm(y_low, right)
    inner = 6.0 * wide - mm(y_low, inner.astype(BF))
    return coef * (4.0 * wide - mm(y_low, inner.astype(BF)))


def tile_any(acts_all, block, prevs, prev_a, owners, damping, init_scale, block_index, cols):
    own, total = lax.axis_index("own"), acts_all.shape[0]
    in_width = prev_a[0].shape[0]
    slot = lax.axis_index("dp") % (lax.axis_size("dp") // lax.axis_size("own"))
    tokens = ((0,), (0,))
    outs, terms, begin = [], [], 0
    for linear in range(2):
        fa, fg, width, c = 2 * linear, 2 * linear + 1, prevs[linear].shape[0], cols[linear]
        a_l = acts_all[:, linear * in_width:(linear + 1) * in_width]
        g_l = block[:, begin:begin + width]
        g_damped = damp(prevs[linear].astype(F32), mm(g_l, g_l, tokens) / total, owners[1, fg], damping[fg])
        g_inv = inverse_columns(g_damped, init_scale[fg, block_index], slot * c, c)
        low = (mm(a_l, g_l, tokens) / total).astype(BF)
        right = mm(low, g_inv).astype(BF)
        a_damped = damp(prev_a[linear], mm(a_l, a_l, tokens) / total, owners[1, fa], damping[fa])
        precond = apply_inverse(a_damped, init_scale[fa, own], right)
        terms.append(jnp.sum(precond * lax.dynamic_slice_in_dim(low, slot * c, c, 1).astype(F32)))
        outs.append(precond)
        begin += width
    return outs[0], outs[1], jnp.broadcast_to(jnp.stack(terms)[:, None], (2, 128))


def gather_fast(acts, grads, prev_low):
    dp, own = lax.axis_index("dp"), lax.axis_index("own")
    z, x = dp // 2, own // 2
    rows, cols = grads.shape
    piece = rows // 4
    both = ("dp", "own")
    at = lambda d, o: d * 4 + o
    dp_swap = lambda m: [(d, d ^ m) for d in range(8)]
    own_swap = lambda m: [(o, o ^ m) for o in range(4)]

    split = lax.all_to_all(grads.reshape(4, piece, cols), "own", 0, 0, tiled=True)
    order = [jnp.bitwise_xor(own, q) for q in (0, 2, 1, 3)]
    mine = jnp.concatenate([lax.dynamic_slice_in_dim(acts, piece * q, piece, 0) for q in order], 0).T
    chunks = {0: mine}
    for m in (2, 4, 6):
        chunks[m] = lax.ppermute(mine, "dp", dp_swap(m))
    for m in (0, 2, 4, 6):
        chunks[m + 1] = lax.ppermute(chunks[m], "dp", dp_swap(1))

    wanted = jnp.broadcast_to(split[:, None], (4, 2, piece, cols)).reshape(8, piece, cols)
    first = lax.all_to_all(wanted, "dp", 0, 0, tiled=True).reshape(8 * piece, cols)
    second = lax.ppermute(first, "own", own_swap(2))
    blocks = [first, second, lax.ppermute(first, "own", own_swap(1)), lax.ppermute(second, "own", own_swap(1))]

    low_bit = (own & 1) == (z & 1)
    prevs = []
    for p in prev_low:
        q = lax.ppermute(p, both, [(at(d, d // 2), at(d, (d // 2) ^ 2)) for d in range(8)])
        p = jnp.where(x == z // 2, p, q)
        q = lax.ppermute(
            p, both, [(at(d, o), at(d, o ^ 1)) for d in range(8) for o in range(4) if (o & 1) == ((d // 2) & 1)]
        )
        prevs.append(jnp.where(low_bit, p, q))
    return [chunks[m] for m in range(8)], blocks, prevs


def gather_any(acts, grads, prev_low, block_index):
    dp_count, own_count = lax.axis_size("dp"), lax.axis_size("own")
    rows, cols = grads.shape
    acts_all = lax.all_gather(acts, "dp", axis=0, tiled=True)
    split = lax.all_to_all(grads.reshape(own_count, rows // own_count, cols), "own", 0, 0, tiled=True)
    wanted = jnp.repeat(split, dp_count // own_count, axis=0)
    pieces = lax.all_to_all(wanted, "dp", 0, 0, tiled=True)
    block = lax.all_gather(pieces, "own", axis=1, tiled=True).reshape(rows * dp_count, cols)
    prevs = [
        lax.dynamic_index_in_dim(lax.all_gather(p[None], "own", axis=0, tiled=True), block_index, 0, keepdims=False)
        for p in prev_low
    ]
    return acts_all, block, prevs


def shards(acts_kv, grads_kv, acts_up, grads_up, prev_a_kv, prev_g_kv, prev_a_up, prev_g_up, owners, damping,
           init_scale, weights_kv, weights_up, step_size):
    dp_count, own_count = lax.axis_size("dp"), lax.axis_size("own")
    dp, own = lax.axis_index("dp"), lax.axis_index("own")
    block_index = dp * own_count // dp_count
    slot = dp % (dp_count // own_count)
    total = acts_kv.shape[0] * dp_count
    cols = (weights_kv.shape[1], weights_up.shape[1])
    entries = tuple(float(w.shape[0] * w.shape[1] * dp_count * own_count) for w in (weights_kv, weights_up))

    acts = jnp.concatenate([acts_kv, acts_up], 1)
    grads = jnp.concatenate([grads_kv, grads_up], 1)
    prev_low = [prev_g_kv[0].astype(BF), prev_g_up[0].astype(BF)]
    prev_a = (prev_a_kv[0], prev_a_up[0])
    if (dp_count, own_count) == (8, 4):
        parts, blocks, prevs = gather_fast(acts, grads, prev_low)
        fresh = owners[1] == 1
        scale = jnp.where(
            lax.broadcasted_iota(jnp.int32, (4,), 0) % 2 == 1,
            lax.dynamic_index_in_dim(init_scale, block_index, 1, keepdims=False),
            lax.dynamic_index_in_dim(init_scale, own, 1, keepdims=False),
        )
        sc = jnp.stack(
            [jnp.where(fresh, 0.5, 1.0), jnp.where(fresh, 0.5 / total, 0.0), damping, scale, jnp.full((4,), 1.0 / total)]
        )
        p_kv, p_up, terms = tile(
            sc, jnp.stack([dp, slot]).astype(jnp.int32), parts, blocks, *prev_a, *prevs, cols
        )
    else:
        acts_all, block, prevs = gather_any(acts, grads, prev_low, block_index)
        p_kv, p_up, terms = tile_any(acts_all, block, prevs, prev_a, owners, damping, init_scale, block_index, cols)
    sent = jnp.broadcast_to(terms.reshape(1, 256), (dp_count * own_count, 256))
    sums = lax.all_to_all(sent, ("dp", "own"), 0, 0, tiled=True)
    return update(entries, step_size, sums, p_kv, p_up, weights_kv, weights_up)


def solution(mesh):
    tok, fac, rep = P("dp", "own"), P("own", None, None), P()
    return jax.shard_map(
        shards,
        mesh=mesh,
        in_specs=(tok, tok, tok, tok, fac, fac, fac, fac, rep, rep, rep, P("own", "dp"), P("own", "dp"), rep),
        out_specs=(P("own", "dp"), P("own", "dp")),
        check_vma=False,
    )
```

```python
import functools

import jax
import jax.numpy as jnp
from jax import lax
from jax.experimental import pallas as pl
from jax.experimental.pallas import tpu as pltpu
from jax.sharding import PartitionSpec as P

BF = jnp.bfloat16
F32 = jnp.float32


def contract(a, b, ad, bd):
    return lax.dot_general(a, b, (((ad,), (bd,)), ((), ())), preferred_element_type=F32)


def tiles(n, step=256):
    return [(s, min(step, n - s)) for s in range(0, n, step)]


def damped_into(m_ref, product, prev_ref, keep, mix, lam):
    n = m_ref.shape[0]
    total = jnp.zeros((1, 1), F32)
    for s, w in tiles(n):
        m = keep * prev_ref[:, s:s + w].astype(F32) + mix * product(s, w)
        rows = lax.broadcasted_iota(jnp.int32, (n, w), 0)
        cols = lax.broadcasted_iota(jnp.int32, (n, w), 1) + s
        m = jnp.where(rows == cols, m + lam, m)
        m_ref[:, s:s + w] = m
        total = total + jnp.sum(m * m, keepdims=True)
    return total


def scaled_into(y_ref, m_ref, coef):
    for s, w in tiles(m_ref.shape[0]):
        y_ref[:, s:s + w] = (coef * m_ref[:, s:s + w]).astype(BF)


def tile_kernel(count, quarters, in_width, widths, sc, where_ref, *refs):
    parts, blocks = refs[:count], refs[count:count + 2 * quarters]
    refs = refs[count + 2 * quarters:]
    prev_kv, prev_up, packed, o_kv, o_up, t_ref = refs[:6]
    at, g, m_a, y_a, low, rt = refs[6:12]
    factor_refs = refs[12:18]
    pg_kv, pg_up, pa_kv, pa_up, packed_in, g_sems, p_sems, a_sems = refs[18:]
    slot = where_ref[0]
    chunk = parts[0].shape[1]
    piece = chunk // quarters
    loads_g, loads_a = [], []
    for m in range(count):
        for q in range(quarters):
            k = m % (count // 2)
            loads_g.append(
                pltpu.make_async_copy(
                    blocks[q + quarters * (2 * m // count)].at[piece * k:piece * (k + 1), :],
                    g.at[chunk * m + piece * q:chunk * m + piece * (q + 1), :],
                    g_sems.at[quarters * m + q],
                )
            )
        loads_a.append(pltpu.make_async_copy(parts[m], at.at[:, chunk * m:chunk * (m + 1)], a_sems.at[m]))
    loads_p = [
        pltpu.make_async_copy(source, target, p_sems.at[i])
        for i, (source, target) in enumerate(((packed, packed_in), (prev_kv, pa_kv), (prev_up, pa_up)))
    ]
    for load in loads_p[:1] + loads_g + loads_a + loads_p[1:]:
        load.start()
    small, half = pg_kv.shape[0], pg_up.shape[0] // 2
    loads_p[0].wait()
    pg_kv[...] = packed_in[half:half + small, :small]
    pg_up[:half, :] = packed_in[:half, :]
    pg_up[half:, half:] = packed_in[half:, half:]
    pg_up[half:, :half] = packed_in[:half, half:].T
    for load in loads_g:
        load.wait()

    begin = 0
    for linear, (pa, pg, out) in enumerate(((pa_kv, pg_kv, o_kv), (pa_up, pg_up, o_up))):
        width, cols = widths[linear], out.shape[1]
        m_g, y_g, i_g = factor_refs[3 * linear:3 * linear + 3]
        fa, fg = 2 * linear, 2 * linear + 1
        part = lambda s, w, begin=begin: g[:, begin + s:begin + s + w]
        squares = damped_into(
            m_g, lambda s, w: contract(part(0, width), part(s, w), 0, 0), pg, sc[0, fg], sc[1, fg], sc[2, fg]
        )
        coef = sc[3, fg] * lax.rsqrt(squares)
        scaled_into(y_g, m_g, coef)
        first = pl.multiple_of(slot * cols, 128)
        for s, w in tiles(cols):
            yc = coef * m_g[:, pl.ds(pl.multiple_of(first + s, 128), w)]
            square = contract(y_g[...], yc.astype(BF), 1, 0)
            cubic = contract(y_g[...], (4.0 * yc - square).astype(BF), 1, 0)
            rows = lax.broadcasted_iota(jnp.int32, (width, w), 0)
            lanes = lax.broadcasted_iota(jnp.int32, (width, w), 1) + (first + s)
            i_g[:, s:s + w] = (coef * (jnp.where(rows == lanes, 4.0, 0.0) - 6.0 * yc + cubic)).astype(BF)
        if linear == 0:
            for load in loads_a:
                load.wait()
        al = at.at[in_width * linear:in_width * (linear + 1), :]
        for s, w in tiles(width):
            low[:, s:s + w] = (contract(al[...], part(s, w), 1, 0) * sc[4, 0]).astype(BF)
        for s, w in tiles(cols):
            rt[:, s:s + w] = contract(low[:, :width], i_g[:, s:s + w], 1, 0).astype(BF)
        loads_p[1 + linear].wait()
        squares = damped_into(
            m_a, lambda s, w: contract(al[...], al[s:s + w, :], 1, 1), pa, sc[0, fa], sc[1, fa], sc[2, fa]
        )
        coef = sc[3, fa] * lax.rsqrt(squares)
        scaled_into(y_a, m_a, coef)
        total = jnp.zeros((1, 1), F32)
        for s, w in tiles(cols):
            right = rt[:, s:s + w]
            wide = right.astype(F32)
            inner = 4.0 * wide - contract(y_a[...], right, 1, 0)
            inner = 6.0 * wide - contract(y_a[...], inner.astype(BF), 1, 0)
            pre = coef * (4.0 * wide - contract(y_a[...], inner.astype(BF), 1, 0))
            out[:, s:s + w] = pre
            own_low = low[:, pl.ds(pl.multiple_of(first + s, 128), w)].astype(F32)
            total = total + jnp.sum(pre * own_low, keepdims=True)
        t_ref[linear:linear + 1, :] = jnp.broadcast_to(total, (1, 128))
        begin += width


def tile(sc, where, parts, blocks, pa_kv, pa_up, packed, widths, cols):
    count, quarters = len(parts), len(blocks) // 2
    in_width = pa_kv.shape[0]
    tokens = parts[0].shape[1] * count
    vmem, smem = pl.BlockSpec(memory_space=pltpu.VMEM), pl.BlockSpec(memory_space=pltpu.SMEM)
    anywhere = pl.BlockSpec(memory_space=pl.ANY)
    factors = []
    for w, c in zip(widths, cols):
        factors += [pltpu.VMEM((w, w), F32), pltpu.VMEM((w, w), BF), pltpu.VMEM((w, c), BF)]
    return pl.pallas_call(
        functools.partial(tile_kernel, count, quarters, in_width, widths),
        out_shape=(
            jax.ShapeDtypeStruct((in_width, cols[0]), F32),
            jax.ShapeDtypeStruct((in_width, cols[1]), F32),
            jax.ShapeDtypeStruct((2, 128), F32),
        ),
        in_specs=[smem, smem] + [anywhere] * (count + 2 * quarters + 3),
        out_specs=(vmem, vmem, vmem),
        scratch_shapes=[
            pltpu.VMEM((2 * in_width, tokens), BF),
            pltpu.VMEM((tokens, sum(widths)), BF),
            pltpu.VMEM((in_width, in_width), F32),
            pltpu.VMEM((in_width, in_width), BF),
            pltpu.VMEM((in_width, max(widths)), BF),
            pltpu.VMEM((in_width, max(cols)), BF),
        ]
        + factors
        + [pltpu.VMEM((w, w), BF) for w in widths]
        + [pltpu.VMEM((in_width, in_width), F32)] * 2
        + [pltpu.VMEM(packed.shape, BF)]
        + [pltpu.SemaphoreType.DMA((n,)) for n in (count * quarters, 3, count)],
        compiler_params=pltpu.CompilerParams(vmem_limit_bytes=32 * 2**20),
        name="tile",
    )(sc, where, *parts, *blocks, pa_kv, pa_up, packed)


def stack_kernel(*refs):
    *sources, out = refs
    rows = sources[0].shape[0]
    z = lax.axis_index("dp") // 2
    inner = (z == 1) | (z == 2)
    for i in range(2):
        out[rows * i:rows * (i + 1), :] = sources[i][...]
        out[rows * (2 + i):rows * (3 + i), :] = jnp.where(inner, sources[3 - i][...], sources[2 + i][...])


def stack_rows(parts):
    rows, cols = parts[0].shape
    vmem = pl.BlockSpec(memory_space=pltpu.VMEM)
    return pl.pallas_call(
        stack_kernel,
        out_shape=jax.ShapeDtypeStruct((rows * len(parts), cols), parts[0].dtype),
        in_specs=[vmem] * len(parts),
        out_specs=vmem,
        name="stack",
    )(*parts)


def update_kernel(entries, step_ref, sums_ref, p_kv, p_up, w_kv, w_up, n_kv, n_up):
    totals = jnp.sum(sums_ref[...], axis=0, keepdims=True)
    for linear, (p, w, n) in enumerate(((p_kv, w_kv, n_kv), (p_up, w_up, n_up))):
        total = totals[:, 128 * linear:128 * (linear + 1)]
        factor = step_ref[0] * jnp.sqrt(entries[linear] / total)
        for s, width in tiles(p.shape[1], 128):
            n[:, s:s + width] = w[:, s:s + width] - factor[:, :width] * p[:, s:s + width]


def update(entries, step_size, sums, p_kv, p_up, w_kv, w_up):
    vmem, smem = pl.BlockSpec(memory_space=pltpu.VMEM), pl.BlockSpec(memory_space=pltpu.SMEM)
    return pl.pallas_call(
        functools.partial(update_kernel, entries),
        out_shape=(jax.ShapeDtypeStruct(w_kv.shape, F32), jax.ShapeDtypeStruct(w_up.shape, F32)),
        in_specs=[smem] + [vmem] * 5,
        out_specs=(vmem, vmem),
        name="update",
    )(step_size.reshape(1), sums, p_kv, p_up, w_kv, w_up)


def mm(a, b, dims=((1,), (0,))):
    return lax.dot_general(a, b, (dims, ((), ())), preferred_element_type=F32)


def damp(previous, stat, fresh, lam):
    n = previous.shape[0]
    eye = lax.broadcasted_iota(jnp.int32, (n, n), 0) == lax.broadcasted_iota(jnp.int32, (n, n), 1)
    mixed = jnp.where(fresh == 1, 0.5 * previous + 0.5 * stat, previous)
    return mixed + jnp.where(eye, lam, 0.0)


def normalised(damped, scale):
    coef = scale / jnp.sqrt(jnp.sum(damped * damped))
    return coef, coef * damped


def inverse_columns(damped, scale, start, width):
    n = damped.shape[0]
    coef, y_full = normalised(damped, scale)
    y_low = y_full.astype(BF)
    y_cols = lax.dynamic_slice_in_dim(y_full, start, width, 1)
    square = mm(y_low, y_cols.astype(BF))
    cubic = mm(y_low, (4.0 * y_cols - square).astype(BF))
    rows = lax.broadcasted_iota(jnp.int32, (n, width), 0)
    cols = lax.broadcasted_iota(jnp.int32, (n, width), 1) + start
    out = coef * (jnp.where(rows == cols, 4.0, 0.0) - 6.0 * y_cols + cubic)
    return out.astype(BF)


def apply_inverse(damped, scale, right):
    coef, y_full = normalised(damped, scale)
    y_low = y_full.astype(BF)
    wide = right.astype(F32)
    inner = 4.0 * wide - mm(y_low, right)
    inner = 6.0 * wide - mm(y_low, inner.astype(BF))
    return coef * (4.0 * wide - mm(y_low, inner.astype(BF)))


def tile_any(acts_all, block, prevs, prev_a, owners, damping, init_scale, block_index, cols):
    own, total = lax.axis_index("own"), acts_all.shape[0]
    in_width = prev_a[0].shape[0]
    slot = lax.axis_index("dp") % (lax.axis_size("dp") // lax.axis_size("own"))
    tokens = ((0,), (0,))
    outs, terms, begin = [], [], 0
    for linear in range(2):
        fa, fg, width, c = 2 * linear, 2 * linear + 1, prevs[linear].shape[0], cols[linear]
        a_l = acts_all[:, linear * in_width:(linear + 1) * in_width]
        g_l = block[:, begin:begin + width]
        g_damped = damp(prevs[linear].astype(F32), mm(g_l, g_l, tokens) / total, owners[1, fg], damping[fg])
        g_inv = inverse_columns(g_damped, init_scale[fg, block_index], slot * c, c)
        low = (mm(a_l, g_l, tokens) / total).astype(BF)
        right = mm(low, g_inv).astype(BF)
        a_damped = damp(prev_a[linear], mm(a_l, a_l, tokens) / total, owners[1, fa], damping[fa])
        precond = apply_inverse(a_damped, init_scale[fa, own], right)
        terms.append(jnp.sum(precond * lax.dynamic_slice_in_dim(low, slot * c, c, 1).astype(F32)))
        outs.append(precond)
        begin += width
    return outs[0], outs[1], jnp.broadcast_to(jnp.stack(terms)[:, None], (2, 128))


def gather_fast(acts, grads, prev_low):
    dp, own = lax.axis_index("dp"), lax.axis_index("own")
    z, x = dp // 2, own // 2
    rows, cols = grads.shape
    piece = rows // 4
    both = ("dp", "own")
    at = lambda d, o: d * 4 + o
    dp_swap = lambda m: [(d, d ^ m) for d in range(8)]
    own_swap = lambda m: [(o, o ^ m) for o in range(4)]

    order = [jnp.bitwise_xor(own, q) for q in (0, 2, 1, 3)]
    mine = jnp.concatenate([lax.dynamic_slice_in_dim(acts, piece * q, piece, 0) for q in order], 0).T

    def along_z(value, pairs):
        return lax.ppermute(value, "dp", [(2 * s + y, 2 * t + y) for s, t in pairs for y in range(2)])

    def across_y(value):
        return lax.ppermute(value, "dp", dp_swap(1))

    def repeat_y(value):
        return jnp.broadcast_to(value[:, None], (4, 2, piece, cols)).reshape(8, piece, cols)

    sends_x = [(at(d, d // 2), at(d, (d // 2) ^ 2)) for d in range(8)]
    sends_core = [(at(d, o), at(d, o ^ 1)) for d in range(8) for o in range(4) if (o & 1) == ((d // 2) & 1)]
    inner = (z == 1) | (z == 2)
    middle, outward = ((1, 2), (2, 1)), ((1, 0), (2, 3))
    pairs, mirror = ((0, 1), (1, 0), (2, 3), (3, 2)), ((0, 3), (3, 0), (1, 2), (2, 1))
    skip = ((0, 2), (2, 0), (1, 3), (3, 1))
    phase = lax.optimization_barrier

    split = lax.all_to_all(grads.reshape(4, piece, cols), "own", 0, 0, tiled=True)
    near, cross_a, beside = along_z(mine, pairs), along_z(mine, middle), across_y(mine)
    split, near, cross_a, beside, prev_low = phase((split, near, cross_a, beside, prev_low))

    wanted = [lax.dynamic_index_in_dim(split, jnp.bitwise_xor(z, k), 0, keepdims=False) for k in range(4)]
    rows_z = [wanted[0]] + [along_z(wanted[k], [(s, s ^ k) for s in range(4)]) for k in (1, 2, 3)]
    far_a = jnp.where(inner, cross_a, along_z(cross_a, outward))
    cross_b = along_z(near, middle)
    near_y = across_y(near)
    prev_x = lax.ppermute(prev_low, both, sends_x)
    rows_z, far_a, cross_b, near_y, prev_x = phase((rows_z, far_a, cross_b, near_y, prev_x))

    strip = stack_rows(rows_z)
    strip_y = across_y(strip)
    far_b = jnp.where(inner, cross_b, along_z(cross_b, outward))
    far_a_y = across_y(far_a)
    prev_low = jnp.where(x == z // 2, prev_low, prev_x)
    strip_y, far_b = phase((strip_y, far_b))

    prev_core = lax.ppermute(prev_low, both, sends_core)
    prev_low = jnp.where((own & 1) == (z & 1), prev_low, prev_core)
    far_b_y = across_y(far_b)
    blocks = []
    for v in (strip, strip_y):
        w = lax.ppermute(v, "own", own_swap(2))
        blocks += [v, w, lax.ppermute(v, "own", own_swap(1)), lax.ppermute(w, "own", own_swap(1))]
    return [mine, near, far_a, far_b, beside, near_y, far_a_y, far_b_y], blocks, prev_low


def gather_any(acts, grads, prev_low, block_index):
    dp_count, own_count = lax.axis_size("dp"), lax.axis_size("own")
    rows, cols = grads.shape
    acts_all = lax.all_gather(acts, "dp", axis=0, tiled=True)
    split = lax.all_to_all(grads.reshape(own_count, rows // own_count, cols), "own", 0, 0, tiled=True)
    wanted = jnp.repeat(split, dp_count // own_count, axis=0)
    pieces = lax.all_to_all(wanted, "dp", 0, 0, tiled=True)
    block = lax.all_gather(pieces, "own", axis=1, tiled=True).reshape(rows * dp_count, cols)
    prevs = [
        lax.dynamic_index_in_dim(lax.all_gather(p[None], "own", axis=0, tiled=True), block_index, 0, keepdims=False)
        for p in prev_low
    ]
    return acts_all, block, prevs


def shards(acts_kv, grads_kv, acts_up, grads_up, prev_a_kv, prev_g_kv, prev_a_up, prev_g_up, owners, damping,
           init_scale, weights_kv, weights_up, step_size):
    dp_count, own_count = lax.axis_size("dp"), lax.axis_size("own")
    dp, own = lax.axis_index("dp"), lax.axis_index("own")
    block_index = dp * own_count // dp_count
    slot = dp % (dp_count // own_count)
    total = acts_kv.shape[0] * dp_count
    cols = (weights_kv.shape[1], weights_up.shape[1])
    entries = tuple(float(w.shape[0] * w.shape[1] * dp_count * own_count) for w in (weights_kv, weights_up))

    acts = jnp.concatenate([acts_kv, acts_up], 1)
    grads = jnp.concatenate([grads_kv, grads_up], 1)
    prev_g = [prev_g_kv[0].astype(BF), prev_g_up[0].astype(BF)]
    prev_a = (prev_a_kv[0], prev_a_up[0])
    if (dp_count, own_count) == (8, 4):
        packed = lax.dynamic_update_slice(prev_g[1], prev_g[0], (prev_g[1].shape[0] // 2, 0))
        parts, blocks, packed = gather_fast(acts, grads, packed)
        fresh = owners[1] == 1
        scale = jnp.where(
            lax.broadcasted_iota(jnp.int32, (4,), 0) % 2 == 1,
            lax.dynamic_index_in_dim(init_scale, block_index, 1, keepdims=False),
            lax.dynamic_index_in_dim(init_scale, own, 1, keepdims=False),
        )
        sc = jnp.stack(
            [jnp.where(fresh, 0.5, 1.0), jnp.where(fresh, 0.5 / total, 0.0), damping, scale, jnp.full((4,), 1.0 / total)]
        )
        p_kv, p_up, terms = tile(
            sc, slot[None].astype(jnp.int32), parts, blocks, *prev_a, packed,
            tuple(p.shape[0] for p in prev_g), cols
        )
    else:
        acts_all, block, prevs = gather_any(acts, grads, prev_g, block_index)
        p_kv, p_up, terms = tile_any(acts_all, block, prevs, prev_a, owners, damping, init_scale, block_index, cols)
    sent = jnp.broadcast_to(terms.reshape(1, 256), (dp_count * own_count, 256))
    sums = lax.all_to_all(sent, ("dp", "own"), 0, 0, tiled=True)
    return update(entries, step_size, sums, p_kv, p_up, weights_kv, weights_up)


def solution(mesh):
    tok, fac, rep = P("dp", "own"), P("own", None, None), P()
    return jax.shard_map(
        shards,
        mesh=mesh,
        in_specs=(tok, tok, tok, tok, fac, fac, fac, fac, rep, rep, rep, P("own", "dp"), P("own", "dp"), rep),
        out_specs=(P("own", "dp"), P("own", "dp")),
        check_vma=False,
    )
```

```python
import functools

import jax
import jax.numpy as jnp
from jax import lax
from jax.experimental import pallas as pl
from jax.experimental.pallas import tpu as pltpu
from jax.sharding import PartitionSpec as P

BF = jnp.bfloat16
F32 = jnp.float32


def contract(a, b, ad, bd):
    return lax.dot_general(a, b, (((ad,), (bd,)), ((), ())), preferred_element_type=F32)


def tiles(n, step=256):
    return [(s, min(step, n - s)) for s in range(0, n, step)]


def damped_into(m_ref, product, prev_ref, keep, mix, lam):
    n = m_ref.shape[0]
    total = jnp.zeros((1, 1), F32)
    for s, w in tiles(n):
        m = keep * prev_ref[:, s:s + w].astype(F32) + mix * product(s, w)
        rows = lax.broadcasted_iota(jnp.int32, (n, w), 0)
        cols = lax.broadcasted_iota(jnp.int32, (n, w), 1) + s
        m = jnp.where(rows == cols, m + lam, m)
        m_ref[:, s:s + w] = m
        total = total + jnp.sum(m * m, keepdims=True)
    return total


def scaled_into(y_ref, m_ref, coef):
    for s, w in tiles(m_ref.shape[0]):
        y_ref[:, s:s + w] = (coef * m_ref[:, s:s + w]).astype(BF)


def tile_kernel(count, quarters, in_width, widths, sc, where_ref, *refs):
    parts, blocks = refs[:count], refs[count:count + 2 * quarters]
    refs = refs[count + 2 * quarters:]
    prev_kv, prev_up, packed, to_kv, to_up, t_ref = refs[:6]
    at, g, m_a, y_a, low, rt = refs[6:12]
    factor_refs = refs[12:18]
    pg_kv, pg_up, pa_kv, pa_up, packed_in, o_kv, o_up, g_sems, p_sems, a_sems, o_sems = refs[18:]
    slot = where_ref[0]
    chunk = parts[0].shape[1]
    z = lax.axis_index("dp") // 2
    inner = ((z == 1) | (z == 2)).astype(jnp.int32)
    origins = [jnp.bitwise_xor(z, k) for k in (0, 1, 2 + inner, 3 - inner)]
    loads_g = [
        pltpu.make_async_copy(blocks[quarters * row + q], g.at[row, :, q], g_sems.at[quarters * row + q])
        for row in range(2)
        for q in range(quarters)
    ]
    loads_a = []
    for m in range(count):
        lane = pl.multiple_of((count // 2 * (m // (count // 2)) + origins[m % (count // 2)]) * chunk, chunk)
        loads_a.append(pltpu.make_async_copy(parts[m], at.at[:, pl.ds(lane, chunk)], a_sems.at[m]))
    loads_p = [
        pltpu.make_async_copy(source, target, p_sems.at[i])
        for i, (source, target) in enumerate(((packed, packed_in), (prev_kv, pa_kv), (prev_up, pa_up)))
    ]
    for load in loads_p[:1] + loads_g + loads_a + loads_p[1:]:
        load.start()
    small, half = pg_kv.shape[0], pg_up.shape[0] // 2
    loads_p[0].wait()
    pg_kv[...] = packed_in[half:half + small, :small]
    pg_up[:half, :] = packed_in[:half, :]
    pg_up[half:, half:] = packed_in[half:, half:]
    pg_up[half:, :half] = packed_in[:half, half:].T
    for load in loads_g:
        load.wait()

    begin, stores = 0, []
    for linear, (pa, pg, out) in enumerate(((pa_kv, pg_kv, o_kv), (pa_up, pg_up, o_up))):
        width, cols = widths[linear], out.shape[1]
        m_g, y_g, i_g = factor_refs[3 * linear:3 * linear + 3]
        fa, fg = 2 * linear, 2 * linear + 1
        part = lambda s, w, begin=begin: g[:, :, :, :, begin + s:begin + s + w].reshape(-1, w)
        squares = damped_into(
            m_g, lambda s, w: contract(part(0, width), part(s, w), 0, 0), pg, sc[0, fg], sc[1, fg], sc[2, fg]
        )
        coef = sc[3, fg] * lax.rsqrt(squares)
        scaled_into(y_g, m_g, coef)
        first = pl.multiple_of(slot * cols, 128)
        for s, w in tiles(cols):
            yc = coef * m_g[:, pl.ds(pl.multiple_of(first + s, 128), w)]
            square = contract(y_g[...], yc.astype(BF), 1, 0)
            cubic = contract(y_g[...], (4.0 * yc - square).astype(BF), 1, 0)
            rows = lax.broadcasted_iota(jnp.int32, (width, w), 0)
            lanes = lax.broadcasted_iota(jnp.int32, (width, w), 1) + (first + s)
            i_g[:, s:s + w] = (coef * (jnp.where(rows == lanes, 4.0, 0.0) - 6.0 * yc + cubic)).astype(BF)
        if linear == 0:
            for load in loads_a:
                load.wait()
        al = at.at[in_width * linear:in_width * (linear + 1), :]
        for s, w in tiles(width):
            low[:, s:s + w] = (contract(al[...], part(s, w), 1, 0) * sc[4, 0]).astype(BF)
        for s, w in tiles(cols):
            rt[:, s:s + w] = contract(low[:, :width], i_g[:, s:s + w], 1, 0).astype(BF)
        loads_p[1 + linear].wait()
        squares = damped_into(
            m_a, lambda s, w: contract(al[...], al[s:s + w, :], 1, 1), pa, sc[0, fa], sc[1, fa], sc[2, fa]
        )
        coef = sc[3, fa] * lax.rsqrt(squares)
        scaled_into(y_a, m_a, coef)
        total = jnp.zeros((1, 1), F32)
        for s, w in tiles(cols):
            right = rt[:, s:s + w]
            wide = right.astype(F32)
            inner = 4.0 * wide - contract(y_a[...], right, 1, 0)
            inner = 6.0 * wide - contract(y_a[...], inner.astype(BF), 1, 0)
            pre = coef * (4.0 * wide - contract(y_a[...], inner.astype(BF), 1, 0))
            out[:, s:s + w] = pre
            own_low = low[:, pl.ds(pl.multiple_of(first + s, 128), w)].astype(F32)
            total = total + jnp.sum(pre * own_low, keepdims=True)
        t_ref[:, :, 128 * linear:128 * (linear + 1)] = jnp.broadcast_to(total[None], (t_ref.shape[0], 1, 128))
        stores.append(pltpu.make_async_copy(out, (to_kv, to_up)[linear], o_sems.at[linear]))
        stores[-1].start()
        begin += width
    for store in stores:
        store.wait()


def tile(devices, sc, where, parts, blocks, pa_kv, pa_up, packed, widths, cols):
    count, quarters = len(parts), len(blocks) // 2
    in_width = pa_kv.shape[0]
    tokens = parts[0].shape[1] * count
    vmem, smem = pl.BlockSpec(memory_space=pltpu.VMEM), pl.BlockSpec(memory_space=pltpu.SMEM)
    anywhere = pl.BlockSpec(memory_space=pl.ANY)
    factors = []
    for w, c in zip(widths, cols):
        factors += [pltpu.VMEM((w, w), F32), pltpu.VMEM((w, w), BF), pltpu.VMEM((w, c), BF)]
    return pl.pallas_call(
        functools.partial(tile_kernel, count, quarters, in_width, widths),
        out_shape=(
            jax.ShapeDtypeStruct((in_width, cols[0]), F32),
            jax.ShapeDtypeStruct((in_width, cols[1]), F32),
            jax.ShapeDtypeStruct((devices, 1, 256), F32),
        ),
        in_specs=[smem, smem] + [anywhere] * (count + 2 * quarters + 3),
        out_specs=(pl.BlockSpec(memory_space=pltpu.HBM),) * 2 + (vmem,),
        scratch_shapes=[
            pltpu.VMEM((2 * in_width, tokens), BF),
            pltpu.VMEM((2, count // 2, quarters, tokens // (count * quarters), sum(widths)), BF),
            pltpu.VMEM((in_width, in_width), F32),
            pltpu.VMEM((in_width, in_width), BF),
            pltpu.VMEM((in_width, max(widths)), BF),
            pltpu.VMEM((in_width, max(cols)), BF),
        ]
        + factors
        + [pltpu.VMEM((w, w), BF) for w in widths]
        + [pltpu.VMEM((in_width, in_width), F32)] * 2
        + [pltpu.VMEM(packed.shape, BF)]
        + [pltpu.VMEM((in_width, c), F32) for c in cols]
        + [pltpu.SemaphoreType.DMA((n,)) for n in (2 * quarters, 3, count, 2)],
        compiler_params=pltpu.CompilerParams(vmem_limit_bytes=32 * 2**20),
        name="tile",
    )(sc, where, *parts, *blocks, pa_kv, pa_up, packed)


def turn_kernel(kv_ref, up_ref, g_kv, g_up, out_ref, g_ref):
    own = lax.axis_index("own")
    rows, width = kv_ref.shape
    piece = rows // 4
    edge = g_kv.shape[1]
    g_ref[:, :edge] = g_kv[...]
    g_ref[:, edge:] = g_up[...]
    for i, ref in enumerate((kv_ref, up_ref)):
        for s, w in tiles(width):
            quarters = [
                ref[pl.ds(pl.multiple_of(jnp.bitwise_xor(own, q) * piece, piece), piece), s:s + w] for q in (0, 2, 1, 3)
            ]
            out_ref[width * i + s:width * i + s + w, :] = jnp.concatenate(quarters, 0).T


def turned(acts, grads):
    rows, width = acts[0].shape
    vmem = pl.BlockSpec(memory_space=pltpu.VMEM)
    return pl.pallas_call(
        turn_kernel,
        out_shape=(
            jax.ShapeDtypeStruct((2 * width, rows), BF),
            jax.ShapeDtypeStruct((rows, sum(v.shape[1] for v in grads)), BF),
        ),
        in_specs=[vmem] * 4,
        out_specs=(vmem, vmem),
        name="turn",
    )(*acts, *grads)


def update_kernel(entries, step_ref, sums_any, p_kv, p_up, w_kv, w_up, n_kv, n_up, sums, *refs):
    values, (sums_sem, load_sems, store_sems) = refs[:6], refs[6:]
    sums_load = pltpu.make_async_copy(sums_any, sums, sums_sem)
    sums_load.start()
    jobs = []
    for linear, (p, w, n) in enumerate(((p_kv, w_kv, n_kv), (p_up, w_up, n_up))):
        for s, width in tiles(p.shape[1], 128):
            part, at = len(jobs), (slice(None), slice(s, s + width))
            p_in, w_in, out = (v.at[at] for v in values[3 * linear:3 * linear + 3])
            loads = [
                pltpu.make_async_copy(p.at[at], p_in, load_sems.at[2 * part]),
                pltpu.make_async_copy(w.at[at], w_in, load_sems.at[2 * part + 1]),
            ]
            for load in loads:
                load.start()
            jobs.append((linear, loads, p_in, w_in, out, pltpu.make_async_copy(out, n.at[at], store_sems.at[part])))
    sums_load.wait()
    totals = jnp.sum(sums[...], axis=0)
    factors = [step_ref[0] * jnp.sqrt(entries[i] / totals[:, 128 * i:128 * (i + 1)]) for i in range(2)]
    for linear, loads, p_in, w_in, out, store in jobs:
        for load in loads:
            load.wait()
        out[...] = w_in[...] - factors[linear][:, :out.shape[1]] * p_in[...]
        store.start()
    for job in jobs:
        job[-1].wait()


def update(entries, step_size, sums, p_kv, p_up, w_kv, w_up):
    smem, anywhere = pl.BlockSpec(memory_space=pltpu.SMEM), pl.BlockSpec(memory_space=pl.ANY)
    hbm = pl.BlockSpec(memory_space=pltpu.HBM)
    parts = sum(len(tiles(w.shape[1], 128)) for w in (w_kv, w_up))
    return pl.pallas_call(
        functools.partial(update_kernel, entries),
        out_shape=(jax.ShapeDtypeStruct(w_kv.shape, F32), jax.ShapeDtypeStruct(w_up.shape, F32)),
        in_specs=[smem, anywhere, hbm, hbm, hbm, hbm],
        out_specs=(hbm, hbm),
        scratch_shapes=[pltpu.VMEM(sums.shape, F32)]
        + [pltpu.VMEM(w.shape, F32) for w in (w_kv, w_up) for _ in range(3)]
        + [pltpu.SemaphoreType.DMA, pltpu.SemaphoreType.DMA((2 * parts,)), pltpu.SemaphoreType.DMA((parts,))],
        name="update",
    )(step_size.reshape(1), sums, p_kv, p_up, w_kv, w_up)


def mm(a, b, dims=((1,), (0,))):
    return lax.dot_general(a, b, (dims, ((), ())), preferred_element_type=F32)


def damp(previous, stat, fresh, lam):
    n = previous.shape[0]
    eye = lax.broadcasted_iota(jnp.int32, (n, n), 0) == lax.broadcasted_iota(jnp.int32, (n, n), 1)
    mixed = jnp.where(fresh == 1, 0.5 * previous + 0.5 * stat, previous)
    return mixed + jnp.where(eye, lam, 0.0)


def normalised(damped, scale):
    coef = scale / jnp.sqrt(jnp.sum(damped * damped))
    return coef, coef * damped


def inverse_columns(damped, scale, start, width):
    n = damped.shape[0]
    coef, y_full = normalised(damped, scale)
    y_low = y_full.astype(BF)
    y_cols = lax.dynamic_slice_in_dim(y_full, start, width, 1)
    square = mm(y_low, y_cols.astype(BF))
    cubic = mm(y_low, (4.0 * y_cols - square).astype(BF))
    rows = lax.broadcasted_iota(jnp.int32, (n, width), 0)
    cols = lax.broadcasted_iota(jnp.int32, (n, width), 1) + start
    out = coef * (jnp.where(rows == cols, 4.0, 0.0) - 6.0 * y_cols + cubic)
    return out.astype(BF)


def apply_inverse(damped, scale, right):
    coef, y_full = normalised(damped, scale)
    y_low = y_full.astype(BF)
    wide = right.astype(F32)
    inner = 4.0 * wide - mm(y_low, right)
    inner = 6.0 * wide - mm(y_low, inner.astype(BF))
    return coef * (4.0 * wide - mm(y_low, inner.astype(BF)))


def tile_any(acts_all, block, prevs, prev_a, owners, damping, init_scale, block_index, cols):
    own, total = lax.axis_index("own"), acts_all.shape[0]
    in_width = prev_a[0].shape[0]
    slot = lax.axis_index("dp") % (lax.axis_size("dp") // lax.axis_size("own"))
    tokens = ((0,), (0,))
    outs, terms, begin = [], [], 0
    for linear in range(2):
        fa, fg, width, c = 2 * linear, 2 * linear + 1, prevs[linear].shape[0], cols[linear]
        a_l = acts_all[:, linear * in_width:(linear + 1) * in_width]
        g_l = block[:, begin:begin + width]
        g_damped = damp(prevs[linear].astype(F32), mm(g_l, g_l, tokens) / total, owners[1, fg], damping[fg])
        g_inv = inverse_columns(g_damped, init_scale[fg, block_index], slot * c, c)
        low = (mm(a_l, g_l, tokens) / total).astype(BF)
        right = mm(low, g_inv).astype(BF)
        a_damped = damp(prev_a[linear], mm(a_l, a_l, tokens) / total, owners[1, fa], damping[fa])
        precond = apply_inverse(a_damped, init_scale[fa, own], right)
        terms.append(jnp.sum(precond * lax.dynamic_slice_in_dim(low, slot * c, c, 1).astype(F32)))
        outs.append(precond)
        begin += width
    return outs[0], outs[1], jnp.broadcast_to(jnp.stack(terms)[:, None], (2, 128))


def gather_fast(acts, grads, prev_low):
    dp, own = lax.axis_index("dp"), lax.axis_index("own")
    z, x = dp // 2, own // 2
    mine, grads = turned(acts, grads)
    rows, cols = grads.shape
    piece = rows // 4
    both = ("dp", "own")
    at = lambda d, o: d * 4 + o
    dp_swap = lambda m: [(d, d ^ m) for d in range(8)]
    own_swap = lambda m: [(o, o ^ m) for o in range(4)]


    def along_z(value, pairs):
        return lax.ppermute(value, "dp", [(2 * s + y, 2 * t + y) for s, t in pairs for y in range(2)])

    def across_y(value):
        return lax.ppermute(value, "dp", dp_swap(1))

    def repeat_y(value):
        return jnp.broadcast_to(value[:, None], (4, 2, piece, cols)).reshape(8, piece, cols)

    sends_x = [(at(d, d // 2), at(d, (d // 2) ^ 2)) for d in range(8)]
    sends_core = [(at(d, o), at(d, o ^ 1)) for d in range(8) for o in range(4) if (o & 1) == ((d // 2) & 1)]
    inner = (z == 1) | (z == 2)
    middle, outward = ((1, 2), (2, 1)), ((1, 0), (2, 3))
    pairs, mirror = ((0, 1), (1, 0), (2, 3), (3, 2)), ((0, 3), (3, 0), (1, 2), (2, 1))
    skip = ((0, 2), (2, 0), (1, 3), (3, 1))
    phase = lax.optimization_barrier

    split = lax.all_to_all(grads.reshape(4, piece, cols), "own", 0, 0, tiled=True)
    near, cross_a, beside = along_z(mine, pairs), along_z(mine, middle), across_y(mine)
    split, near, cross_a, beside, prev_low = phase((split, near, cross_a, beside, prev_low))

    z_lines = [[2 * s + y for s in range(4)] for y in range(2)]
    strip = lax.all_to_all(split, "dp", 0, 0, tiled=True, axis_index_groups=z_lines)
    far_a = jnp.where(inner, cross_a, along_z(cross_a, outward))
    cross_b = along_z(near, middle)
    near_y = across_y(near)
    prev_x = lax.ppermute(prev_low, both, sends_x)
    strip, far_a, cross_b, near_y, prev_x = phase((strip, far_a, cross_b, near_y, prev_x))

    strip_y = across_y(strip)
    far_a_y = across_y(far_a)
    far_b = jnp.where(inner, cross_b, along_z(cross_b, outward))
    strip_x = lax.ppermute(strip, "own", own_swap(2))
    prev_low = jnp.where(x == z // 2, prev_low, prev_x)
    prev_core = lax.ppermute(prev_low, both, sends_core)
    strip, strip_y, far_b = phase((strip, strip_y, far_b))

    far_b_y = across_y(far_b)
    strip_xy = lax.ppermute(strip_y, "own", own_swap(2))
    prev_low = jnp.where((own & 1) == (z & 1), prev_low, prev_core)
    blocks = []
    for v, w in ((strip, strip_x), (strip_y, strip_xy)):
        blocks += [v, w, lax.ppermute(v, "own", own_swap(1)), lax.ppermute(w, "own", own_swap(1))]
    return [mine, near, far_a, far_b, beside, near_y, far_a_y, far_b_y], blocks, prev_low


def gather_any(acts, grads, prev_low, block_index):
    dp_count, own_count = lax.axis_size("dp"), lax.axis_size("own")
    grads = jnp.concatenate(grads, 1)
    rows, cols = grads.shape
    acts_all = lax.all_gather(jnp.concatenate(acts, 1), "dp", axis=0, tiled=True)
    split = lax.all_to_all(grads.reshape(own_count, rows // own_count, cols), "own", 0, 0, tiled=True)
    wanted = jnp.repeat(split, dp_count // own_count, axis=0)
    pieces = lax.all_to_all(wanted, "dp", 0, 0, tiled=True)
    block = lax.all_gather(pieces, "own", axis=1, tiled=True).reshape(rows * dp_count, cols)
    prevs = [
        lax.dynamic_index_in_dim(lax.all_gather(p[None], "own", axis=0, tiled=True), block_index, 0, keepdims=False)
        for p in prev_low
    ]
    return acts_all, block, prevs


def shards(acts_kv, grads_kv, acts_up, grads_up, prev_a_kv, prev_g_kv, prev_a_up, prev_g_up, owners, damping,
           init_scale, weights_kv, weights_up, step_size):
    dp_count, own_count = lax.axis_size("dp"), lax.axis_size("own")
    dp, own = lax.axis_index("dp"), lax.axis_index("own")
    block_index = dp * own_count // dp_count
    slot = dp % (dp_count // own_count)
    total = acts_kv.shape[0] * dp_count
    cols = (weights_kv.shape[1], weights_up.shape[1])
    entries = tuple(float(w.shape[0] * w.shape[1] * dp_count * own_count) for w in (weights_kv, weights_up))

    acts = (acts_kv, acts_up)
    grads = (grads_kv, grads_up)
    prev_g = [prev_g_kv[0].astype(BF), prev_g_up[0].astype(BF)]
    prev_a = (prev_a_kv[0], prev_a_up[0])
    if (dp_count, own_count) == (8, 4):
        packed = lax.dynamic_update_slice(prev_g[1], prev_g[0], (prev_g[1].shape[0] // 2, 0))
        parts, blocks, packed = gather_fast(acts, grads, packed)
        fresh = owners[1] == 1
        scale = jnp.where(
            lax.broadcasted_iota(jnp.int32, (4,), 0) % 2 == 1,
            lax.dynamic_index_in_dim(init_scale, block_index, 1, keepdims=False),
            lax.dynamic_index_in_dim(init_scale, own, 1, keepdims=False),
        )
        sc = jnp.stack(
            [jnp.where(fresh, 0.5, 1.0), jnp.where(fresh, 0.5 / total, 0.0), damping, scale, jnp.full((4,), 1.0 / total)]
        )
        p_kv, p_up, sent = tile(
            dp_count * own_count, sc, slot[None].astype(jnp.int32), parts, blocks, *prev_a, packed,
            tuple(p.shape[0] for p in prev_g), cols
        )
    else:
        acts_all, block, prevs = gather_any(acts, grads, prev_g, block_index)
        p_kv, p_up, terms = tile_any(acts_all, block, prevs, prev_a, owners, damping, init_scale, block_index, cols)
        sent = jnp.broadcast_to(terms.reshape(1, 1, 256), (dp_count * own_count, 1, 256))
    sums = lax.all_to_all(sent, ("dp", "own"), 0, 0, tiled=True)
    return update(entries, step_size, sums, p_kv, p_up, weights_kv, weights_up)


def solution(mesh):
    tok, fac, rep = P("dp", "own"), P("own", None, None), P()
    return jax.shard_map(
        shards,
        mesh=mesh,
        in_specs=(tok, tok, tok, tok, fac, fac, fac, fac, rep, rep, rep, P("own", "dp"), P("own", "dp"), rep),
        out_specs=(P("own", "dp"), P("own", "dp")),
        check_vma=False,
    )
```

```python
import functools

import jax
import jax.numpy as jnp
from jax import lax
from jax.experimental import pallas as pl
from jax.experimental.pallas import tpu as pltpu
from jax.sharding import PartitionSpec as P

BF = jnp.bfloat16
F32 = jnp.float32


def contract(a, b, ad, bd):
    return lax.dot_general(a, b, (((ad,), (bd,)), ((), ())), preferred_element_type=F32)


def tiles(n, step=256):
    return [(s, min(step, n - s)) for s in range(0, n, step)]


def damped_into(m_ref, product, prev_ref, keep, mix, lam):
    n = m_ref.shape[0]
    total = jnp.zeros((1, 1), F32)
    for s, w in tiles(n):
        m = keep * prev_ref[:, s:s + w].astype(F32) + mix * product(s, w)
        rows = lax.broadcasted_iota(jnp.int32, (n, w), 0)
        cols = lax.broadcasted_iota(jnp.int32, (n, w), 1) + s
        m = jnp.where(rows == cols, m + lam, m)
        m_ref[:, s:s + w] = m
        total = total + jnp.sum(m * m, keepdims=True)
    return total


def scaled_into(y_ref, m_ref, coef):
    for s, w in tiles(m_ref.shape[0]):
        y_ref[:, s:s + w] = (coef * m_ref[:, s:s + w]).astype(BF)


def tile_kernel(count, quarters, in_width, widths, sc, where_ref, *refs):
    parts, blocks = refs[:count], refs[count:count + 2 * quarters]
    refs = refs[count + 2 * quarters:]
    prev_kv, prev_up, packed, to_kv, to_up, t_ref = refs[:6]
    at, g, m_a, y_a, low, rt = refs[6:12]
    factor_refs = refs[12:18]
    pg_kv, pg_up, pa_kv, pa_up, packed_in, o_kv, o_up, g_sems, p_sems, a_sems, o_sems = refs[18:]
    slot = where_ref[0]
    chunk = parts[0].shape[1]
    z = lax.axis_index("dp") // 2
    inner = ((z == 1) | (z == 2)).astype(jnp.int32)
    origins = [jnp.bitwise_xor(z, k) for k in (0, 1, 2 + inner, 3 - inner)]
    loads_g = [
        pltpu.make_async_copy(blocks[quarters * row + q], g.at[row, :, q], g_sems.at[quarters * row + q])
        for row in range(2)
        for q in range(quarters)
    ]
    loads_a = []
    for m in range(count):
        lane = pl.multiple_of((count // 2 * (m // (count // 2)) + origins[m % (count // 2)]) * chunk, chunk)
        loads_a.append(pltpu.make_async_copy(parts[m], at.at[:, pl.ds(lane, chunk)], a_sems.at[m]))
    loads_p = [
        pltpu.make_async_copy(source, target, p_sems.at[i])
        for i, (source, target) in enumerate(((packed, packed_in), (prev_kv, pa_kv), (prev_up, pa_up)))
    ]
    for load in loads_p[:1] + loads_g + loads_a + loads_p[1:]:
        load.start()
    small, half = pg_kv.shape[0], pg_up.shape[0] // 2
    loads_p[0].wait()
    pg_kv[...] = packed_in[half:half + small, :small]
    pg_up[:half, :] = packed_in[:half, :]
    pg_up[half:, half:] = packed_in[half:, half:]
    pg_up[half:, :half] = packed_in[:half, half:].T
    for load in loads_g:
        load.wait()

    begin, stores = 0, []
    for linear, (pa, pg, out) in enumerate(((pa_kv, pg_kv, o_kv), (pa_up, pg_up, o_up))):
        width, cols = widths[linear], out.shape[1]
        m_g, y_g, i_g = factor_refs[3 * linear:3 * linear + 3]
        fa, fg = 2 * linear, 2 * linear + 1
        part = lambda s, w, begin=begin: g[:, :, :, :, begin + s:begin + s + w].reshape(-1, w)
        squares = damped_into(
            m_g, lambda s, w: contract(part(0, width), part(s, w), 0, 0), pg, sc[0, fg], sc[1, fg], sc[2, fg]
        )
        coef = sc[3, fg] * lax.rsqrt(squares)
        scaled_into(y_g, m_g, coef)
        first = pl.multiple_of(slot * cols, 128)
        for s, w in tiles(cols, 512):
            yc = coef * m_g[:, pl.ds(pl.multiple_of(first + s, 128), w)]
            square = contract(y_g[...], yc.astype(BF), 1, 0)
            cubic = contract(y_g[...], (4.0 * yc - square).astype(BF), 1, 0)
            rows = lax.broadcasted_iota(jnp.int32, (width, w), 0)
            lanes = lax.broadcasted_iota(jnp.int32, (width, w), 1) + (first + s)
            i_g[:, s:s + w] = (coef * (jnp.where(rows == lanes, 4.0, 0.0) - 6.0 * yc + cubic)).astype(BF)
        if linear == 0:
            for load in loads_a:
                load.wait()
        al = at.at[in_width * linear:in_width * (linear + 1), :]
        for s, w in tiles(width):
            low[:, s:s + w] = (contract(al[...], part(s, w), 1, 0) * sc[4, 0]).astype(BF)
        for s, w in tiles(cols, 512):
            rt[:, s:s + w] = contract(low[:, :width], i_g[:, s:s + w], 1, 0).astype(BF)
        loads_p[1 + linear].wait()
        squares = damped_into(
            m_a, lambda s, w: contract(al[...], al[s:s + w, :], 1, 1), pa, sc[0, fa], sc[1, fa], sc[2, fa]
        )
        coef = sc[3, fa] * lax.rsqrt(squares)
        scaled_into(y_a, m_a, coef)
        total = jnp.zeros((1, 1), F32)
        for s, w in tiles(cols, 512):
            right = rt[:, s:s + w]
            wide = right.astype(F32)
            inner = 4.0 * wide - contract(y_a[...], right, 1, 0)
            inner = 6.0 * wide - contract(y_a[...], inner.astype(BF), 1, 0)
            pre = coef * (4.0 * wide - contract(y_a[...], inner.astype(BF), 1, 0))
            out[:, s:s + w] = pre
            own_low = low[:, pl.ds(pl.multiple_of(first + s, 128), w)].astype(F32)
            total = total + jnp.sum(pre * own_low, keepdims=True)
        t_ref[:, :, 128 * linear:128 * (linear + 1)] = jnp.broadcast_to(total[None], (t_ref.shape[0], 1, 128))
        stores.append(pltpu.make_async_copy(out, (to_kv, to_up)[linear], o_sems.at[linear]))
        stores[-1].start()
        begin += width
    for store in stores:
        store.wait()


def tile(devices, sc, where, parts, blocks, pa_kv, pa_up, packed, widths, cols):
    count, quarters = len(parts), len(blocks) // 2
    in_width = pa_kv.shape[0]
    tokens = parts[0].shape[1] * count
    vmem, smem = pl.BlockSpec(memory_space=pltpu.VMEM), pl.BlockSpec(memory_space=pltpu.SMEM)
    anywhere = pl.BlockSpec(memory_space=pl.ANY)
    factors = []
    for w, c in zip(widths, cols):
        factors += [pltpu.VMEM((w, w), F32), pltpu.VMEM((w, w), BF), pltpu.VMEM((w, c), BF)]
    return pl.pallas_call(
        functools.partial(tile_kernel, count, quarters, in_width, widths),
        out_shape=(
            jax.ShapeDtypeStruct((in_width, cols[0]), F32),
            jax.ShapeDtypeStruct((in_width, cols[1]), F32),
            jax.ShapeDtypeStruct((devices, 1, 256), F32),
        ),
        in_specs=[smem, smem] + [anywhere] * (count + 2 * quarters + 3),
        out_specs=(pl.BlockSpec(memory_space=pltpu.HBM),) * 2 + (vmem,),
        scratch_shapes=[
            pltpu.VMEM((2 * in_width, tokens), BF),
            pltpu.VMEM((2, count // 2, quarters, tokens // (count * quarters), sum(widths)), BF),
            pltpu.VMEM((in_width, in_width), F32),
            pltpu.VMEM((in_width, in_width), BF),
            pltpu.VMEM((in_width, max(widths)), BF),
            pltpu.VMEM((in_width, max(cols)), BF),
        ]
        + factors
        + [pltpu.VMEM((w, w), BF) for w in widths]
        + [pltpu.VMEM((in_width, in_width), F32)] * 2
        + [pltpu.VMEM(packed.shape, BF)]
        + [pltpu.VMEM((in_width, c), F32) for c in cols]
        + [pltpu.SemaphoreType.DMA((n,)) for n in (2 * quarters, 3, count, 2)],
        compiler_params=pltpu.CompilerParams(vmem_limit_bytes=48 * 2**20),
        name="tile",
    )(sc, where, *parts, *blocks, pa_kv, pa_up, packed)


def turn_kernel(kv_ref, up_ref, g_kv, g_up, out_ref, g_ref):
    own = lax.axis_index("own")
    rows, width = kv_ref.shape
    piece = rows // 4
    edge = g_kv.shape[1]
    g_ref[:, :edge] = g_kv[...]
    g_ref[:, edge:] = g_up[...]
    for i, ref in enumerate((kv_ref, up_ref)):
        for s, w in tiles(width):
            quarters = [
                ref[pl.ds(pl.multiple_of(jnp.bitwise_xor(own, q) * piece, piece), piece), s:s + w] for q in (0, 2, 1, 3)
            ]
            out_ref[width * i + s:width * i + s + w, :] = jnp.concatenate(quarters, 0).T


def turned(acts, grads):
    rows, width = acts[0].shape
    vmem = pl.BlockSpec(memory_space=pltpu.VMEM)
    return pl.pallas_call(
        turn_kernel,
        out_shape=(
            jax.ShapeDtypeStruct((2 * width, rows), BF),
            jax.ShapeDtypeStruct((rows, sum(v.shape[1] for v in grads)), BF),
        ),
        in_specs=[vmem] * 4,
        out_specs=(vmem, vmem),
        name="turn",
    )(*acts, *grads)


def update_kernel(entries, step_ref, sums_any, p_kv, p_up, w_kv, w_up, n_kv, n_up, sums, *refs):
    values, (sums_sem, load_sems, store_sems) = refs[:6], refs[6:]
    sums_load = pltpu.make_async_copy(sums_any, sums, sums_sem)
    sums_load.start()
    jobs = []
    for linear, (p, w, n) in enumerate(((p_kv, w_kv, n_kv), (p_up, w_up, n_up))):
        for s, width in tiles(p.shape[1], 128):
            part, at = len(jobs), (slice(None), slice(s, s + width))
            p_in, w_in, out = (v.at[at] for v in values[3 * linear:3 * linear + 3])
            loads = [
                pltpu.make_async_copy(p.at[at], p_in, load_sems.at[2 * part]),
                pltpu.make_async_copy(w.at[at], w_in, load_sems.at[2 * part + 1]),
            ]
            for load in loads:
                load.start()
            jobs.append((linear, loads, p_in, w_in, out, pltpu.make_async_copy(out, n.at[at], store_sems.at[part])))
    sums_load.wait()
    totals = jnp.sum(sums[...], axis=0)
    factors = [step_ref[0] * jnp.sqrt(entries[i] / totals[:, 128 * i:128 * (i + 1)]) for i in range(2)]
    for linear, loads, p_in, w_in, out, store in jobs:
        for load in loads:
            load.wait()
        out[...] = w_in[...] - factors[linear][:, :out.shape[1]] * p_in[...]
        store.start()
    for job in jobs:
        job[-1].wait()


def update(entries, step_size, sums, p_kv, p_up, w_kv, w_up):
    smem, anywhere = pl.BlockSpec(memory_space=pltpu.SMEM), pl.BlockSpec(memory_space=pl.ANY)
    hbm = pl.BlockSpec(memory_space=pltpu.HBM)
    parts = sum(len(tiles(w.shape[1], 128)) for w in (w_kv, w_up))
    return pl.pallas_call(
        functools.partial(update_kernel, entries),
        out_shape=(jax.ShapeDtypeStruct(w_kv.shape, F32), jax.ShapeDtypeStruct(w_up.shape, F32)),
        in_specs=[smem, anywhere, hbm, hbm, hbm, hbm],
        out_specs=(hbm, hbm),
        scratch_shapes=[pltpu.VMEM(sums.shape, F32)]
        + [pltpu.VMEM(w.shape, F32) for w in (w_kv, w_up) for _ in range(3)]
        + [pltpu.SemaphoreType.DMA, pltpu.SemaphoreType.DMA((2 * parts,)), pltpu.SemaphoreType.DMA((parts,))],
        name="update",
    )(step_size.reshape(1), sums, p_kv, p_up, w_kv, w_up)


def mm(a, b, dims=((1,), (0,))):
    return lax.dot_general(a, b, (dims, ((), ())), preferred_element_type=F32)


def damp(previous, stat, fresh, lam):
    n = previous.shape[0]
    eye = lax.broadcasted_iota(jnp.int32, (n, n), 0) == lax.broadcasted_iota(jnp.int32, (n, n), 1)
    mixed = jnp.where(fresh == 1, 0.5 * previous + 0.5 * stat, previous)
    return mixed + jnp.where(eye, lam, 0.0)


def normalised(damped, scale):
    coef = scale / jnp.sqrt(jnp.sum(damped * damped))
    return coef, coef * damped


def inverse_columns(damped, scale, start, width):
    n = damped.shape[0]
    coef, y_full = normalised(damped, scale)
    y_low = y_full.astype(BF)
    y_cols = lax.dynamic_slice_in_dim(y_full, start, width, 1)
    square = mm(y_low, y_cols.astype(BF))
    cubic = mm(y_low, (4.0 * y_cols - square).astype(BF))
    rows = lax.broadcasted_iota(jnp.int32, (n, width), 0)
    cols = lax.broadcasted_iota(jnp.int32, (n, width), 1) + start
    out = coef * (jnp.where(rows == cols, 4.0, 0.0) - 6.0 * y_cols + cubic)
    return out.astype(BF)


def apply_inverse(damped, scale, right):
    coef, y_full = normalised(damped, scale)
    y_low = y_full.astype(BF)
    wide = right.astype(F32)
    inner = 4.0 * wide - mm(y_low, right)
    inner = 6.0 * wide - mm(y_low, inner.astype(BF))
    return coef * (4.0 * wide - mm(y_low, inner.astype(BF)))


def tile_any(acts_all, block, prevs, prev_a, owners, damping, init_scale, block_index, cols):
    own, total = lax.axis_index("own"), acts_all.shape[0]
    in_width = prev_a[0].shape[0]
    slot = lax.axis_index("dp") % (lax.axis_size("dp") // lax.axis_size("own"))
    tokens = ((0,), (0,))
    outs, terms, begin = [], [], 0
    for linear in range(2):
        fa, fg, width, c = 2 * linear, 2 * linear + 1, prevs[linear].shape[0], cols[linear]
        a_l = acts_all[:, linear * in_width:(linear + 1) * in_width]
        g_l = block[:, begin:begin + width]
        g_damped = damp(prevs[linear].astype(F32), mm(g_l, g_l, tokens) / total, owners[1, fg], damping[fg])
        g_inv = inverse_columns(g_damped, init_scale[fg, block_index], slot * c, c)
        low = (mm(a_l, g_l, tokens) / total).astype(BF)
        right = mm(low, g_inv).astype(BF)
        a_damped = damp(prev_a[linear], mm(a_l, a_l, tokens) / total, owners[1, fa], damping[fa])
        precond = apply_inverse(a_damped, init_scale[fa, own], right)
        terms.append(jnp.sum(precond * lax.dynamic_slice_in_dim(low, slot * c, c, 1).astype(F32)))
        outs.append(precond)
        begin += width
    return outs[0], outs[1], jnp.broadcast_to(jnp.stack(terms)[:, None], (2, 128))


def gather_fast(acts, grads, prev_low):
    dp, own = lax.axis_index("dp"), lax.axis_index("own")
    z, x = dp // 2, own // 2
    mine, grads = turned(acts, grads)
    rows, cols = grads.shape
    piece = rows // 4
    both = ("dp", "own")
    at = lambda d, o: d * 4 + o
    dp_swap = lambda m: [(d, d ^ m) for d in range(8)]
    own_swap = lambda m: [(o, o ^ m) for o in range(4)]


    def along_z(value, pairs):
        return lax.ppermute(value, "dp", [(2 * s + y, 2 * t + y) for s, t in pairs for y in range(2)])

    def across_y(value):
        return lax.ppermute(value, "dp", dp_swap(1))

    def repeat_y(value):
        return jnp.broadcast_to(value[:, None], (4, 2, piece, cols)).reshape(8, piece, cols)

    sends_x = [(at(d, d // 2), at(d, (d // 2) ^ 2)) for d in range(8)]
    sends_core = [(at(d, o), at(d, o ^ 1)) for d in range(8) for o in range(4) if (o & 1) == ((d // 2) & 1)]
    inner = (z == 1) | (z == 2)
    middle, outward = ((1, 2), (2, 1)), ((1, 0), (2, 3))
    pairs, mirror = ((0, 1), (1, 0), (2, 3), (3, 2)), ((0, 3), (3, 0), (1, 2), (2, 1))
    skip = ((0, 2), (2, 0), (1, 3), (3, 1))
    phase = lax.optimization_barrier

    split = lax.all_to_all(grads.reshape(4, piece, cols), "own", 0, 0, tiled=True)
    near, cross_a, beside = along_z(mine, pairs), along_z(mine, middle), across_y(mine)
    split, near, cross_a, beside, prev_low = phase((split, near, cross_a, beside, prev_low))

    z_lines = [[2 * s + y for s in range(4)] for y in range(2)]
    strip = lax.all_to_all(split, "dp", 0, 0, tiled=True, axis_index_groups=z_lines)
    far_a = jnp.where(inner, cross_a, along_z(cross_a, outward))
    cross_b = along_z(near, middle)
    near_y = across_y(near)
    prev_x = lax.ppermute(prev_low, both, sends_x)
    strip, far_a, cross_b, near_y, prev_x = phase((strip, far_a, cross_b, near_y, prev_x))

    strip_y = across_y(strip)
    far_a_y = across_y(far_a)
    far_b = jnp.where(inner, cross_b, along_z(cross_b, outward))
    strip_x = lax.ppermute(strip, "own", own_swap(2))
    prev_low = jnp.where(x == z // 2, prev_low, prev_x)
    prev_core = lax.ppermute(prev_low, both, sends_core)
    strip, strip_y, far_b = phase((strip, strip_y, far_b))

    far_b_y = across_y(far_b)
    strip_xy = lax.ppermute(strip_y, "own", own_swap(2))
    prev_low = jnp.where((own & 1) == (z & 1), prev_low, prev_core)
    blocks = []
    for v, w in ((strip, strip_x), (strip_y, strip_xy)):
        blocks += [v, w, lax.ppermute(v, "own", own_swap(1)), lax.ppermute(w, "own", own_swap(1))]
    return [mine, near, far_a, far_b, beside, near_y, far_a_y, far_b_y], blocks, prev_low


def gather_any(acts, grads, prev_low, block_index):
    dp_count, own_count = lax.axis_size("dp"), lax.axis_size("own")
    grads = jnp.concatenate(grads, 1)
    rows, cols = grads.shape
    acts_all = lax.all_gather(jnp.concatenate(acts, 1), "dp", axis=0, tiled=True)
    split = lax.all_to_all(grads.reshape(own_count, rows // own_count, cols), "own", 0, 0, tiled=True)
    wanted = jnp.repeat(split, dp_count // own_count, axis=0)
    pieces = lax.all_to_all(wanted, "dp", 0, 0, tiled=True)
    block = lax.all_gather(pieces, "own", axis=1, tiled=True).reshape(rows * dp_count, cols)
    prevs = [
        lax.dynamic_index_in_dim(lax.all_gather(p[None], "own", axis=0, tiled=True), block_index, 0, keepdims=False)
        for p in prev_low
    ]
    return acts_all, block, prevs


def shards(acts_kv, grads_kv, acts_up, grads_up, prev_a_kv, prev_g_kv, prev_a_up, prev_g_up, owners, damping,
           init_scale, weights_kv, weights_up, step_size):
    dp_count, own_count = lax.axis_size("dp"), lax.axis_size("own")
    dp, own = lax.axis_index("dp"), lax.axis_index("own")
    block_index = dp * own_count // dp_count
    slot = dp % (dp_count // own_count)
    total = acts_kv.shape[0] * dp_count
    cols = (weights_kv.shape[1], weights_up.shape[1])
    entries = tuple(float(w.shape[0] * w.shape[1] * dp_count * own_count) for w in (weights_kv, weights_up))

    acts = (acts_kv, acts_up)
    grads = (grads_kv, grads_up)
    prev_g = [prev_g_kv[0].astype(BF), prev_g_up[0].astype(BF)]
    prev_a = (prev_a_kv[0], prev_a_up[0])
    if (dp_count, own_count) == (8, 4):
        packed = lax.dynamic_update_slice(prev_g[1], prev_g[0], (prev_g[1].shape[0] // 2, 0))
        parts, blocks, packed = gather_fast(acts, grads, packed)
        fresh = owners[1] == 1
        scale = jnp.where(
            lax.broadcasted_iota(jnp.int32, (4,), 0) % 2 == 1,
            lax.dynamic_index_in_dim(init_scale, block_index, 1, keepdims=False),
            lax.dynamic_index_in_dim(init_scale, own, 1, keepdims=False),
        )
        sc = jnp.stack(
            [jnp.where(fresh, 0.5, 1.0), jnp.where(fresh, 0.5 / total, 0.0), damping, scale, jnp.full((4,), 1.0 / total)]
        )
        p_kv, p_up, sent = tile(
            dp_count * own_count, sc, slot[None].astype(jnp.int32), parts, blocks, *prev_a, packed,
            tuple(p.shape[0] for p in prev_g), cols
        )
    else:
        acts_all, block, prevs = gather_any(acts, grads, prev_g, block_index)
        p_kv, p_up, terms = tile_any(acts_all, block, prevs, prev_a, owners, damping, init_scale, block_index, cols)
        sent = jnp.broadcast_to(terms.reshape(1, 1, 256), (dp_count * own_count, 1, 256))
    sums = lax.all_to_all(sent, ("dp", "own"), 0, 0, tiled=True)
    return update(entries, step_size, sums, p_kv, p_up, weights_kv, weights_up)


def solution(mesh):
    tok, fac, rep = P("dp", "own"), P("own", None, None), P()
    return jax.shard_map(
        shards,
        mesh=mesh,
        in_specs=(tok, tok, tok, tok, fac, fac, fac, fac, rep, rep, rep, P("own", "dp"), P("own", "dp"), rep),
        out_specs=(P("own", "dp"), P("own", "dp")),
        check_vma=False,
    )
```

```python
import functools

import jax
import jax.numpy as jnp
from jax import lax
from jax.experimental import pallas as pl
from jax.experimental.pallas import tpu as pltpu
from jax.sharding import PartitionSpec as P

BF = jnp.bfloat16
F32 = jnp.float32


def contract(a, b, ad, bd):
    return lax.dot_general(a, b, (((ad,), (bd,)), ((), ())), preferred_element_type=F32)


def tiles(n, step=256):
    return [(s, min(step, n - s)) for s in range(0, n, step)]


def damped_into(m_ref, product, prev_ref, keep, mix, lam):
    n = m_ref.shape[0]
    total = jnp.zeros((1, 1), F32)
    for s, w in tiles(n):
        m = keep * prev_ref[:, s:s + w].astype(F32) + mix * product(s, w)
        rows = lax.broadcasted_iota(jnp.int32, (n, w), 0)
        cols = lax.broadcasted_iota(jnp.int32, (n, w), 1) + s
        m = jnp.where(rows == cols, m + lam, m)
        m_ref[:, s:s + w] = m
        total = total + jnp.sum(m * m, keepdims=True)
    return total


def scaled_into(y_ref, m_ref, coef):
    for s, w in tiles(m_ref.shape[0]):
        y_ref[:, s:s + w] = (coef * m_ref[:, s:s + w]).astype(BF)


def tile_kernel(count, quarters, in_width, widths, sc, where_ref, *refs):
    parts, blocks = refs[:count], refs[count:count + 2 * quarters]
    refs = refs[count + 2 * quarters:]
    prev_kv, prev_up, packed, to_kv, to_up, t_ref = refs[:6]
    at, g, m_a, y_a, low, rt = refs[6:12]
    factor_refs = refs[12:18]
    pg_kv, pg_up, pa_kv, pa_up, packed_in, o_kv, o_up, g_sems, p_sems, a_sems, o_sems = refs[18:]
    slot = where_ref[0]
    chunk = parts[0].shape[1]
    z = lax.axis_index("dp") // 2
    inner = ((z == 1) | (z == 2)).astype(jnp.int32)
    origins = [jnp.bitwise_xor(z, k) for k in (0, 1, 2 + inner, 3 - inner)]
    loads_g = [
        pltpu.make_async_copy(blocks[quarters * row + q], g.at[row, :, q], g_sems.at[quarters * row + q])
        for row in range(2)
        for q in range(quarters)
    ]
    loads_a = []
    for m in range(count):
        lane = pl.multiple_of((count // 2 * (m // (count // 2)) + origins[m % (count // 2)]) * chunk, chunk)
        loads_a.append(pltpu.make_async_copy(parts[m], at.at[:, pl.ds(lane, chunk)], a_sems.at[m]))
    loads_p = [
        pltpu.make_async_copy(source, target, p_sems.at[i])
        for i, (source, target) in enumerate(((packed, packed_in), (prev_kv, pa_kv), (prev_up, pa_up)))
    ]
    for load in loads_p[:1] + loads_g + loads_a + loads_p[1:]:
        load.start()
    small, half = pg_kv.shape[0], pg_up.shape[0] // 2
    loads_p[0].wait()
    pg_kv[...] = packed_in[half:half + small, :small]
    pg_up[:half, :] = packed_in[:half, :]
    pg_up[half:, half:] = packed_in[half:, half:]
    pg_up[half:, :half] = packed_in[:half, half:].T
    for load in loads_g:
        load.wait()

    begin, stores = 0, []
    for linear, (pa, pg, out) in enumerate(((pa_kv, pg_kv, o_kv), (pa_up, pg_up, o_up))):
        width, cols = widths[linear], out.shape[1]
        m_g, y_g, i_g = factor_refs[3 * linear:3 * linear + 3]
        fa, fg = 2 * linear, 2 * linear + 1
        part = lambda s, w, begin=begin: g[:, :, :, :, begin + s:begin + s + w].reshape(-1, w)
        squares = damped_into(
            m_g, lambda s, w: contract(part(0, width), part(s, w), 0, 0), pg, sc[0, fg], sc[1, fg], sc[2, fg]
        )
        coef = sc[3, fg] * lax.rsqrt(squares)
        scaled_into(y_g, m_g, coef)
        first = pl.multiple_of(slot * cols, 128)
        for s, w in tiles(cols, 512):
            yc = coef * m_g[:, pl.ds(pl.multiple_of(first + s, 128), w)]
            square = contract(y_g[...], yc.astype(BF), 1, 0)
            cubic = contract(y_g[...], (4.0 * yc - square).astype(BF), 1, 0)
            rows = lax.broadcasted_iota(jnp.int32, (width, w), 0)
            lanes = lax.broadcasted_iota(jnp.int32, (width, w), 1) + (first + s)
            i_g[:, s:s + w] = (coef * (jnp.where(rows == lanes, 4.0, 0.0) - 6.0 * yc + cubic)).astype(BF)
        if linear == 0:
            for load in loads_a:
                load.wait()
        al = at.at[in_width * linear:in_width * (linear + 1), :]
        for s, w in tiles(width):
            low[:, s:s + w] = (contract(al[...], part(s, w), 1, 0) * sc[4, 0]).astype(BF)
        for s, w in tiles(cols, 512):
            rt[:, s:s + w] = contract(low[:, :width], i_g[:, s:s + w], 1, 0).astype(BF)
        loads_p[1 + linear].wait()
        squares = damped_into(
            m_a, lambda s, w: contract(al[...], al[s:s + w, :], 1, 1), pa, sc[0, fa], sc[1, fa], sc[2, fa]
        )
        coef = sc[3, fa] * lax.rsqrt(squares)
        scaled_into(y_a, m_a, coef)
        total = jnp.zeros((1, 1), F32)
        for s, w in tiles(cols, 512):
            right = rt[:, s:s + w]
            wide = right.astype(F32)
            inner = 4.0 * wide - contract(y_a[...], right, 1, 0)
            inner = 6.0 * wide - contract(y_a[...], inner.astype(BF), 1, 0)
            pre = coef * (4.0 * wide - contract(y_a[...], inner.astype(BF), 1, 0))
            out[:, s:s + w] = pre
            own_low = low[:, pl.ds(pl.multiple_of(first + s, 128), w)].astype(F32)
            total = total + jnp.sum(pre * own_low, keepdims=True)
        t_ref[:, :, 128 * linear:128 * (linear + 1)] = jnp.broadcast_to(total[None], (t_ref.shape[0], 1, 128))
        stores.append(pltpu.make_async_copy(out, (to_kv, to_up)[linear], o_sems.at[linear]))
        stores[-1].start()
        begin += width
    for store in stores:
        store.wait()


def tile(devices, sc, where, parts, blocks, pa_kv, pa_up, packed, widths, cols):
    count, quarters = len(parts), len(blocks) // 2
    in_width = pa_kv.shape[0]
    tokens = parts[0].shape[1] * count
    vmem, smem = pl.BlockSpec(memory_space=pltpu.VMEM), pl.BlockSpec(memory_space=pltpu.SMEM)
    anywhere = pl.BlockSpec(memory_space=pl.ANY)
    factors = []
    for w, c in zip(widths, cols):
        factors += [pltpu.VMEM((w, w), F32), pltpu.VMEM((w, w), BF), pltpu.VMEM((w, c), BF)]
    return pl.pallas_call(
        functools.partial(tile_kernel, count, quarters, in_width, widths),
        out_shape=(
            jax.ShapeDtypeStruct((in_width, cols[0]), F32),
            jax.ShapeDtypeStruct((in_width, cols[1]), F32),
            jax.ShapeDtypeStruct((devices, 1, 256), F32),
        ),
        in_specs=[smem, smem] + [anywhere] * (count + 2 * quarters + 3),
        out_specs=(pl.BlockSpec(memory_space=pltpu.HBM),) * 2 + (vmem,),
        scratch_shapes=[
            pltpu.VMEM((2 * in_width, tokens), BF),
            pltpu.VMEM((2, count // 2, quarters, tokens // (count * quarters), sum(widths)), BF),
            pltpu.VMEM((in_width, in_width), F32),
            pltpu.VMEM((in_width, in_width), BF),
            pltpu.VMEM((in_width, max(widths)), BF),
            pltpu.VMEM((in_width, max(cols)), BF),
        ]
        + factors
        + [pltpu.VMEM((w, w), BF) for w in widths]
        + [pltpu.VMEM((in_width, in_width), F32)] * 2
        + [pltpu.VMEM(packed.shape, BF)]
        + [pltpu.VMEM((in_width, c), F32) for c in cols]
        + [pltpu.SemaphoreType.DMA((n,)) for n in (2 * quarters, 3, count, 2)],
        compiler_params=pltpu.CompilerParams(vmem_limit_bytes=54 * 2**20),
        name="tile",
    )(sc, where, *parts, *blocks, pa_kv, pa_up, packed)


def turn_kernel(kv_ref, up_ref, g_kv, g_up, out_ref, g_ref):
    own = lax.axis_index("own")
    rows, width = kv_ref.shape
    piece = rows // 4
    edge = g_kv.shape[1]
    g_ref[:, :edge] = g_kv[...]
    g_ref[:, edge:] = g_up[...]
    for i, ref in enumerate((kv_ref, up_ref)):
        for s, w in tiles(width):
            quarters = [
                ref[pl.ds(pl.multiple_of(jnp.bitwise_xor(own, q) * piece, piece), piece), s:s + w] for q in (0, 2, 1, 3)
            ]
            out_ref[width * i + s:width * i + s + w, :] = jnp.concatenate(quarters, 0).T


def turned(acts, grads):
    rows, width = acts[0].shape
    vmem = pl.BlockSpec(memory_space=pltpu.VMEM)
    return pl.pallas_call(
        turn_kernel,
        out_shape=(
            jax.ShapeDtypeStruct((2 * width, rows), BF),
            jax.ShapeDtypeStruct((rows, sum(v.shape[1] for v in grads)), BF),
        ),
        in_specs=[vmem] * 4,
        out_specs=(vmem, vmem),
        name="turn",
    )(*acts, *grads)


def update_kernel(entries, step_ref, sums_any, p_kv, p_up, w_kv, w_up, n_kv, n_up, sums, *refs):
    values, (sums_sem, load_sems, store_sems) = refs[:6], refs[6:]
    sums_load = pltpu.make_async_copy(sums_any, sums, sums_sem)
    sums_load.start()
    jobs = []
    for linear, (p, w, n) in enumerate(((p_kv, w_kv, n_kv), (p_up, w_up, n_up))):
        for s, width in tiles(p.shape[1], 128):
            part, at = len(jobs), (slice(None), slice(s, s + width))
            p_in, w_in, out = (v.at[at] for v in values[3 * linear:3 * linear + 3])
            loads = [
                pltpu.make_async_copy(p.at[at], p_in, load_sems.at[2 * part]),
                pltpu.make_async_copy(w.at[at], w_in, load_sems.at[2 * part + 1]),
            ]
            for load in loads:
                load.start()
            jobs.append((linear, loads, p_in, w_in, out, pltpu.make_async_copy(out, n.at[at], store_sems.at[part])))
    sums_load.wait()
    totals = jnp.sum(sums[...], axis=0)
    factors = [step_ref[0] * jnp.sqrt(entries[i] / totals[:, 128 * i:128 * (i + 1)]) for i in range(2)]
    for linear, loads, p_in, w_in, out, store in jobs:
        for load in loads:
            load.wait()
        out[...] = w_in[...] - factors[linear][:, :out.shape[1]] * p_in[...]
        store.start()
    for job in jobs:
        job[-1].wait()


def update(entries, step_size, sums, p_kv, p_up, w_kv, w_up):
    smem, anywhere = pl.BlockSpec(memory_space=pltpu.SMEM), pl.BlockSpec(memory_space=pl.ANY)
    hbm = pl.BlockSpec(memory_space=pltpu.HBM)
    parts = sum(len(tiles(w.shape[1], 128)) for w in (w_kv, w_up))
    return pl.pallas_call(
        functools.partial(update_kernel, entries),
        out_shape=(jax.ShapeDtypeStruct(w_kv.shape, F32), jax.ShapeDtypeStruct(w_up.shape, F32)),
        in_specs=[smem, anywhere, hbm, hbm, hbm, hbm],
        out_specs=(hbm, hbm),
        scratch_shapes=[pltpu.VMEM(sums.shape, F32)]
        + [pltpu.VMEM(w.shape, F32) for w in (w_kv, w_up) for _ in range(3)]
        + [pltpu.SemaphoreType.DMA, pltpu.SemaphoreType.DMA((2 * parts,)), pltpu.SemaphoreType.DMA((parts,))],
        name="update",
    )(step_size.reshape(1), sums, p_kv, p_up, w_kv, w_up)


def mm(a, b, dims=((1,), (0,))):
    return lax.dot_general(a, b, (dims, ((), ())), preferred_element_type=F32)


def damp(previous, stat, fresh, lam):
    n = previous.shape[0]
    eye = lax.broadcasted_iota(jnp.int32, (n, n), 0) == lax.broadcasted_iota(jnp.int32, (n, n), 1)
    mixed = jnp.where(fresh == 1, 0.5 * previous + 0.5 * stat, previous)
    return mixed + jnp.where(eye, lam, 0.0)


def normalised(damped, scale):
    coef = scale / jnp.sqrt(jnp.sum(damped * damped))
    return coef, coef * damped


def inverse_columns(damped, scale, start, width):
    n = damped.shape[0]
    coef, y_full = normalised(damped, scale)
    y_low = y_full.astype(BF)
    y_cols = lax.dynamic_slice_in_dim(y_full, start, width, 1)
    square = mm(y_low, y_cols.astype(BF))
    cubic = mm(y_low, (4.0 * y_cols - square).astype(BF))
    rows = lax.broadcasted_iota(jnp.int32, (n, width), 0)
    cols = lax.broadcasted_iota(jnp.int32, (n, width), 1) + start
    out = coef * (jnp.where(rows == cols, 4.0, 0.0) - 6.0 * y_cols + cubic)
    return out.astype(BF)


def apply_inverse(damped, scale, right):
    coef, y_full = normalised(damped, scale)
    y_low = y_full.astype(BF)
    wide = right.astype(F32)
    inner = 4.0 * wide - mm(y_low, right)
    inner = 6.0 * wide - mm(y_low, inner.astype(BF))
    return coef * (4.0 * wide - mm(y_low, inner.astype(BF)))


def tile_any(acts_all, block, prevs, prev_a, owners, damping, init_scale, block_index, cols):
    own, total = lax.axis_index("own"), acts_all.shape[0]
    in_width = prev_a[0].shape[0]
    slot = lax.axis_index("dp") % (lax.axis_size("dp") // lax.axis_size("own"))
    tokens = ((0,), (0,))
    outs, terms, begin = [], [], 0
    for linear in range(2):
        fa, fg, width, c = 2 * linear, 2 * linear + 1, prevs[linear].shape[0], cols[linear]
        a_l = acts_all[:, linear * in_width:(linear + 1) * in_width]
        g_l = block[:, begin:begin + width]
        g_damped = damp(prevs[linear].astype(F32), mm(g_l, g_l, tokens) / total, owners[1, fg], damping[fg])
        g_inv = inverse_columns(g_damped, init_scale[fg, block_index], slot * c, c)
        low = (mm(a_l, g_l, tokens) / total).astype(BF)
        right = mm(low, g_inv).astype(BF)
        a_damped = damp(prev_a[linear], mm(a_l, a_l, tokens) / total, owners[1, fa], damping[fa])
        precond = apply_inverse(a_damped, init_scale[fa, own], right)
        terms.append(jnp.sum(precond * lax.dynamic_slice_in_dim(low, slot * c, c, 1).astype(F32)))
        outs.append(precond)
        begin += width
    return outs[0], outs[1], jnp.broadcast_to(jnp.stack(terms)[:, None], (2, 128))


def gather_fast(acts, grads, prev_low):
    dp, own = lax.axis_index("dp"), lax.axis_index("own")
    z, x = dp // 2, own // 2
    mine, grads = turned(acts, grads)
    rows, cols = grads.shape
    piece = rows // 4
    both = ("dp", "own")
    at = lambda d, o: d * 4 + o
    dp_swap = lambda m: [(d, d ^ m) for d in range(8)]
    own_swap = lambda m: [(o, o ^ m) for o in range(4)]


    def along_z(value, pairs):
        return lax.ppermute(value, "dp", [(2 * s + y, 2 * t + y) for s, t in pairs for y in range(2)])

    def across_y(value):
        return lax.ppermute(value, "dp", dp_swap(1))

    def repeat_y(value):
        return jnp.broadcast_to(value[:, None], (4, 2, piece, cols)).reshape(8, piece, cols)

    sends_x = [(at(d, d // 2), at(d, (d // 2) ^ 2)) for d in range(8)]
    sends_core = [(at(d, o), at(d, o ^ 1)) for d in range(8) for o in range(4) if (o & 1) == ((d // 2) & 1)]
    inner = (z == 1) | (z == 2)
    middle, outward = ((1, 2), (2, 1)), ((1, 0), (2, 3))
    pairs, mirror = ((0, 1), (1, 0), (2, 3), (3, 2)), ((0, 3), (3, 0), (1, 2), (2, 1))
    skip = ((0, 2), (2, 0), (1, 3), (3, 1))
    phase = lax.optimization_barrier

    split = lax.all_to_all(grads.reshape(4, piece, cols), "own", 0, 0, tiled=True)
    near, cross_a, beside = along_z(mine, pairs), along_z(mine, middle), across_y(mine)
    split, near, cross_a, beside, prev_low = phase((split, near, cross_a, beside, prev_low))

    z_lines = [[2 * s + y for s in range(4)] for y in range(2)]
    strip = lax.all_to_all(split, "dp", 0, 0, tiled=True, axis_index_groups=z_lines)
    far_a = jnp.where(inner, cross_a, along_z(cross_a, outward))
    cross_b = along_z(near, middle)
    near_y = across_y(near)
    prev_x = lax.ppermute(prev_low, both, sends_x)
    far_a_y = across_y(far_a)
    strip, far_a_y, cross_b, near_y, prev_x = phase((strip, far_a_y, cross_b, near_y, prev_x))

    strip_y = across_y(strip)
    far_b = jnp.where(inner, cross_b, along_z(cross_b, outward))
    strip_x = lax.ppermute(strip, "own", own_swap(2))
    prev_low = jnp.where(x == z // 2, prev_low, prev_x)
    prev_core = lax.ppermute(prev_low, both, sends_core)
    strip, strip_y, far_b = phase((strip, strip_y, far_b))

    far_b_y = across_y(far_b)
    strip_xy = lax.ppermute(strip_y, "own", own_swap(2))
    prev_low = jnp.where((own & 1) == (z & 1), prev_low, prev_core)
    blocks = []
    for v, w in ((strip, strip_x), (strip_y, strip_xy)):
        blocks += [v, w, lax.ppermute(v, "own", own_swap(1)), lax.ppermute(w, "own", own_swap(1))]
    return [mine, near, far_a, far_b, beside, near_y, far_a_y, far_b_y], blocks, prev_low


def gather_any(acts, grads, prev_low, block_index):
    dp_count, own_count = lax.axis_size("dp"), lax.axis_size("own")
    grads = jnp.concatenate(grads, 1)
    rows, cols = grads.shape
    acts_all = lax.all_gather(jnp.concatenate(acts, 1), "dp", axis=0, tiled=True)
    split = lax.all_to_all(grads.reshape(own_count, rows // own_count, cols), "own", 0, 0, tiled=True)
    wanted = jnp.repeat(split, dp_count // own_count, axis=0)
    pieces = lax.all_to_all(wanted, "dp", 0, 0, tiled=True)
    block = lax.all_gather(pieces, "own", axis=1, tiled=True).reshape(rows * dp_count, cols)
    prevs = [
        lax.dynamic_index_in_dim(lax.all_gather(p[None], "own", axis=0, tiled=True), block_index, 0, keepdims=False)
        for p in prev_low
    ]
    return acts_all, block, prevs


def shards(acts_kv, grads_kv, acts_up, grads_up, prev_a_kv, prev_g_kv, prev_a_up, prev_g_up, owners, damping,
           init_scale, weights_kv, weights_up, step_size):
    dp_count, own_count = lax.axis_size("dp"), lax.axis_size("own")
    dp, own = lax.axis_index("dp"), lax.axis_index("own")
    block_index = dp * own_count // dp_count
    slot = dp % (dp_count // own_count)
    total = acts_kv.shape[0] * dp_count
    cols = (weights_kv.shape[1], weights_up.shape[1])
    entries = tuple(float(w.shape[0] * w.shape[1] * dp_count * own_count) for w in (weights_kv, weights_up))

    acts = (acts_kv, acts_up)
    grads = (grads_kv, grads_up)
    prev_g = [prev_g_kv[0].astype(BF), prev_g_up[0].astype(BF)]
    prev_a = (prev_a_kv[0], prev_a_up[0])
    if (dp_count, own_count) == (8, 4):
        packed = lax.dynamic_update_slice(prev_g[1], prev_g[0], (prev_g[1].shape[0] // 2, 0))
        parts, blocks, packed = gather_fast(acts, grads, packed)
        fresh = owners[1] == 1
        scale = jnp.where(
            lax.broadcasted_iota(jnp.int32, (4,), 0) % 2 == 1,
            lax.dynamic_index_in_dim(init_scale, block_index, 1, keepdims=False),
            lax.dynamic_index_in_dim(init_scale, own, 1, keepdims=False),
        )
        sc = jnp.stack(
            [jnp.where(fresh, 0.5, 1.0), jnp.where(fresh, 0.5 / total, 0.0), damping, scale, jnp.full((4,), 1.0 / total)]
        )
        p_kv, p_up, sent = tile(
            dp_count * own_count, sc, slot[None].astype(jnp.int32), parts, blocks, *prev_a, packed,
            tuple(p.shape[0] for p in prev_g), cols
        )
    else:
        acts_all, block, prevs = gather_any(acts, grads, prev_g, block_index)
        p_kv, p_up, terms = tile_any(acts_all, block, prevs, prev_a, owners, damping, init_scale, block_index, cols)
        sent = jnp.broadcast_to(terms.reshape(1, 1, 256), (dp_count * own_count, 1, 256))
    sums = lax.all_to_all(sent, ("dp", "own"), 0, 0, tiled=True)
    return update(entries, step_size, sums, p_kv, p_up, weights_kv, weights_up)


def solution(mesh):
    tok, fac, rep = P("dp", "own"), P("own", None, None), P()
    return jax.shard_map(
        shards,
        mesh=mesh,
        in_specs=(tok, tok, tok, tok, fac, fac, fac, fac, rep, rep, rep, P("own", "dp"), P("own", "dp"), rep),
        out_specs=(P("own", "dp"), P("own", "dp")),
        check_vma=False,
    )
```
